256 devices in a mesh: freq: 4 (over z_lo), space: 64 (over x, z_hi, y, core).
Axes of the slice: x: 4, y: 4, z: 8 (z_hi: 2, z_lo: 4; z = z_hi * 4 + z_lo), core: 2. Of those that a mesh axis runs over, the one named last changes fastest.
Arguments:
- wavefields: float32 [2, 4, 2, 2048, 2048], P(None, 'freq', None, 'space'), may hold values from -6 to 6
- frequencies: float32 [4], P('freq'), may hold values from 1.5 to 4
- velocity: float32 [16, 2048, 2048], P('freq', 'space'), may hold values from 1 to 2
- slab_owner: int32 [1], replicated, may hold values from 0 to 15
- ref_velocity: float32 [1, 2], replicated, may hold values from 1 to 2
- ref_index: int32 [1, 128], replicated, may hold values from 0 to 1
Outputs:
- extrapolated: float32 [2, 4, 2, 2048, 2048], P(None, 'freq', None, 'space')
- image: float32 [1, 2048, 2048], P(None, 'space')
The draws below stay inside these ranges and needn't reach their ends.
All inputs are finite; a program needn't handle non-finite values.
Results may differ from the reference program's by a relative error of at most 0.0003.
Values sent between devices are 32-bit elements; how exact they have to be, the bound alone decides.
No kernel may reach another device: no remote copies, remote signals or barrier semaphores. Data moves between devices by JAX's collectives and lax.ppermute only.
A program may use at most 64 MiB of HBM per device.

```python
import math
import jax
import jax.numpy as jnp
from jax import lax

NX = 2048
NY = 2048
DEPTHS = 1
NREF = 2
RB = 16
DZ = 4
NW = 4
SLABS = 16
BLOCKS = 128


def place_ends(values, key, smallest, largest):
    spot = [jax.random.randint(jax.random.fold_in(key, axis), (), 0, length) for axis, length in enumerate(values.shape)]
    longest = values.shape.index(max(values.shape))
    beside = spot[:longest] + [(spot[longest] + 1) % values.shape[longest]] + spot[longest + 1:]
    return values.at[tuple(spot)].set(smallest).at[tuple(beside)].set(largest)


def block_scale(rng, shape, pieces, low, high):
    def one(axis_at, blocks):
        draws = jax.random.uniform(jax.random.fold_in(jax.random.fold_in(rng, 6), axis_at), (blocks,), jnp.float32, low / len(pieces), high / len(pieces))
        return jnp.repeat(jnp.exp(draws), shape[axis_at] // blocks).reshape((-1,) + (1,) * (len(shape) - axis_at - 1))

    gain = one(*pieces[0])
    for cut in pieces[1:]:
        gain = gain * one(*cut)
    return gain


def normal_values(rng, shape, scale, limit, cuts=(), kind=jnp.bfloat16):
    values = scale * jax.random.normal(rng, shape, jnp.float32)
    if cuts:
        values = values * block_scale(rng, shape, cuts, -0.22, 0.18)
    return jnp.clip(values, -limit, limit).astype(kind)


def setup_inputs(seed: int = 0) -> dict:
    key_of = jax.random.split(jax.random.key(seed), 7)
    wavefields = normal_values(key_of[0], (2, NW, 2, NX, NY), 1.0, 6.0, ((1, 4), (3, 64)), jnp.float32)
    frequencies = jnp.clip(jnp.exp(math.log(4.0) - 0.98082925 * jax.random.uniform(key_of[1], (NW,), jnp.float32) ** block_scale(key_of[1], (NW,), ((0, 4),), -0.2, 0.2)), 1.5, 4.0)
    velocity = jnp.clip(1.0 + 1.0 * jax.random.uniform(key_of[2], (SLABS, NX, NY), jnp.float32) ** block_scale(key_of[2], (SLABS, NX, NY), ((0, 4), (1, 64)), -0.2, 0.2), 1.0, 2.0)
    slab_owner = jax.random.randint(key_of[3], (DEPTHS,), 0, SLABS).astype(jnp.int32)
    ref_velocity = jnp.clip(jax.random.uniform(key_of[4], (DEPTHS, NREF), jnp.float32, 1.0, 2.0), 1.0, 2.0)
    ref_index = place_ends(jax.random.randint(key_of[5], (DEPTHS, BLOCKS), 0, NREF), jax.random.fold_in(key_of[5], 1), 0, NREF - 1).astype(jnp.int32)
    return {"wavefields": wavefields, "frequencies": frequencies, "velocity": velocity, "slab_owner": slab_owner, "ref_velocity": ref_velocity, "ref_index": ref_index}


def wave_numbers(length):
    counter = jnp.arange(length, dtype=jnp.int32)
    signed = jnp.where(counter < length // 2, counter, counter - length)
    return 2.0 * jnp.pi / length * signed.astype(jnp.float32)

def reference(wavefields, frequencies, velocity, slab_owner, ref_velocity, ref_index):
    field_signs = jnp.array([-1.0, 1.0], dtype=jnp.float32)[:, None, None]
    squared = wave_numbers(NX)[:, None] ** 2 + wave_numbers(NY)[None, :] ** 2
    fields = jnp.moveaxis(wavefields, 1, 0)
    images = []
    for depth_step in range(DEPTHS):
        slab_speed = velocity[slab_owner[depth_step]]
        row_refs = jnp.repeat(ref_index[depth_step], RB)
        ref_rows = ref_velocity[depth_step][row_refs]

        def advance(packed):
            wave_now, omega_one = packed
            complex_wave = wave_now[:, 0] + 1j * wave_now[:, 1]
            spectrum = jnp.fft.fft2(complex_wave)
            chosen = jnp.zeros_like(complex_wave)
            for ref_slot in range(NREF):
                vertical = (omega_one / ref_velocity[depth_step, ref_slot]) ** 2 - squared
                vertical_root = jnp.sqrt(jnp.abs(vertical))
                shift_phase = jnp.where(vertical >= 0.0, jnp.exp(1j * field_signs * DZ * vertical_root), jnp.exp(-DZ * vertical_root) + 0j)
                returned = jnp.fft.ifft2(spectrum * shift_phase)
                chosen = jnp.where((row_refs == ref_slot)[None, :, None], returned, chosen)
            split_phase = field_signs * omega_one * DZ * (1.0 / slab_speed - 1.0 / ref_rows[:, None])
            chosen = chosen * jnp.exp(1j * split_phase)
            coupling = DZ * (slab_speed - ref_rows[:, None]) * ref_rows[:, None] / (16.0 * omega_one)
            padded = jnp.pad(chosen, ((0, 0), (1, 1), (1, 1)))
            laplace = padded[:, 2:, 1:-1] + padded[:, :-2, 1:-1] + padded[:, 1:-1, 2:] + padded[:, 1:-1, :-2] - 4.0 * chosen
            result = chosen + 1j * field_signs * coupling * laplace
            return jnp.stack([jnp.real(result), jnp.imag(result)], axis=1)
        fields = lax.map(advance, (fields, frequencies))
        images.append(lax.optimization_barrier(jnp.sum(fields[:, 0, 0] * fields[:, 1, 0] + fields[:, 0, 1] * fields[:, 1, 1], axis=0)))
    return (jnp.moveaxis(fields, 0, 1), jnp.stack(images, axis=0))
```

```python
import functools
import math

import jax
import jax.numpy as jnp
import numpy as np
from jax import lax
from jax.experimental import pallas as pl
from jax.experimental.pallas import tpu as pltpu
from jax.sharding import PartitionSpec as P

DZ = 4
INTERPRET = False
VMEM_BYTES = 20 * 2**20
BF16 = jnp.bfloat16

NY_A, NY_B = 16, 128
NX_S, NX_R = 64, 32
NY, NX = NY_A * NY_B, NX_S * NX_R


def split_bf16(matrix):
    high = np.asarray(matrix, np.float32).astype(BF16)
    low = (np.asarray(matrix, np.float64) - high.astype(np.float64)).astype(np.float32).astype(BF16)
    return high, low


@functools.cache
def constants():
    k2 = np.arange(NY_B)
    b = np.arange(NY_B)
    angle = 2.0 * np.pi * (np.outer(k2, b) % NY_B) / NY_B
    cosine, sine = np.cos(angle), np.sin(angle)
    forward = np.stack(
        [np.concatenate([cosine, sine], 1), np.concatenate([-sine, cosine], 1)], 0
    )
    forward = forward.reshape(2, 8, 16, 256).transpose(1, 0, 2, 3).reshape(256, 256)
    inverse = forward.copy() / NY
    fh, fl = split_bf16(forward)
    y_forward = np.concatenate([fh, fl, fh], 1)
    ih, il = split_bf16(inverse)
    y_inverse = np.concatenate([ih, il, ih], 0)
    r = np.arange(NX_R)
    angle = 2.0 * np.pi * (np.outer(r, r) % NX_R) / NX_R
    cosine = np.kron(np.eye(4), np.cos(angle))
    sine = np.kron(np.eye(4), np.sin(angle))
    x_forward = np.block([[cosine, -sine], [sine, cosine]])
    x_inverse = np.block([[cosine, sine], [-sine, cosine]]) / NX
    xh, xl = split_bf16(x_forward)
    x_forward = np.concatenate([xh, xl, xh], 0)
    xh, xl = split_bf16(x_inverse)
    x_inverse = np.concatenate([xh, xl, xh], 0)
    angle = 2.0 * np.pi * np.outer(np.arange(NY_A), b) / NY
    y_twiddle = np.stack([np.cos(angle), -np.sin(angle)]).astype(np.float32)
    angle = 2.0 * np.pi * np.outer(np.arange(NX_S), np.tile(r, 4)) / NX
    x_twiddle = np.stack([np.cos(angle), -np.sin(angle)]).astype(np.float32)
    return dict(
        y_forward=y_forward,
        y_inverse=y_inverse,
        x_forward=x_forward,
        x_inverse=x_inverse,
        y_twiddle=y_twiddle,
        x_twiddle=x_twiddle,
    )


def times(value, numerator, length, sign):
    real, imag = value
    turn = (sign * numerator) % length
    eighth = turn * 8
    if turn == 0:
        return real, imag
    if eighth % length == 0:
        step = eighth // length
        half = math.sqrt(0.5)
        if step == 2:
            return -imag, real
        if step == 4:
            return -real, -imag
        if step == 6:
            return imag, -real
        if step == 1:
            return (real - imag) * half, (real + imag) * half
        if step == 3:
            return (real + imag) * -half, (real - imag) * half
        if step == 5:
            return (imag - real) * half, (real + imag) * -half
        return (real + imag) * half, (imag - real) * half
    cosine = math.cos(2.0 * math.pi * turn / length)
    sine = math.sin(2.0 * math.pi * turn / length)
    return real * cosine - imag * sine, real * sine + imag * cosine


def plus(left, right):
    return left[0] + right[0], left[1] + right[1]


def minus(left, right):
    return left[0] - right[0], left[1] - right[1]


def transform(values, sign):
    length = len(values)
    if length == 1:
        return values
    if length == 2:
        return [plus(values[0], values[1]), minus(values[0], values[1])]
    if length == 4:
        even_sum, even_diff = plus(values[0], values[2]), minus(values[0], values[2])
        odd_sum, odd_diff = plus(values[1], values[3]), minus(values[1], values[3])
        if sign > 0:
            first = (even_diff[0] - odd_diff[1], even_diff[1] + odd_diff[0])
            third = (even_diff[0] + odd_diff[1], even_diff[1] - odd_diff[0])
        else:
            first = (even_diff[0] + odd_diff[1], even_diff[1] - odd_diff[0])
            third = (even_diff[0] - odd_diff[1], even_diff[1] + odd_diff[0])
        return [plus(even_sum, odd_sum), first, minus(even_sum, odd_sum), third]
    radix = 4 if length % 4 == 0 and length > 8 else 2
    rest = length // radix
    columns = [transform(values[i::radix], sign) for i in range(radix)]
    result = [None] * length
    for k in range(rest):
        picked = [times(columns[i][k], i * k, length, sign) for i in range(radix)]
        for q, value in enumerate(transform(picked, sign)):
            result[k + rest * q] = value
    return result


def spread(value):
    high = value.astype(BF16)
    low = (value - high.astype(jnp.float32)).astype(BF16)
    return jnp.concatenate([high, high, low], axis=1)


def matmul(left, right, contract):
    return lax.dot_general(left, right, (contract, ((), ())), preferred_element_type=jnp.float32)


def forward_y_kernel(wave_ref, matrix_ref, twiddle_ref, out_ref, mid_ref):
    for field in range(2):
        for tile in range(4):
            rows = slice(8 * tile, 8 * tile + 8)
            values = [
                tuple(wave_ref[field, 0, c, rows, 128 * a : 128 * a + 128] for c in range(2))
                for a in range(NY_A)
            ]
            for k1, (real, imag) in enumerate(transform(values, -1)):
                if k1:
                    tr, ti = twiddle_ref[0, k1 : k1 + 1, :], twiddle_ref[1, k1 : k1 + 1, :]
                    real, imag = real * tr - imag * ti, real * ti + imag * tr
                at = k1 * 64 + field * 32 + tile * 8
                mid_ref[at : at + 8, 0:128] = real
                mid_ref[at : at + 8, 128:256] = imag
    matrix = matrix_ref[...]
    for pair in range(4):
        packed = spread(mid_ref[256 * pair : 256 * pair + 256, :])
        product = matmul(matrix, packed, ((1,), (1,)))
        for half in range(2):
            at = 16 * pair + 8 * half
            out_ref[at : at + 8] = product[:, 128 * half : 128 * half + 128].reshape(8, 32, 128)


def column_transform(load, store, sign, hold_ref):
    for n0 in range(8):
        piece = transform([load(8 * n1 + n0) for n1 in range(8)], sign)
        for ka in range(8):
            real, imag = times(piece[ka], n0 * ka, 64, sign)
            hold_ref[0, ka * 8 + n0] = real
            hold_ref[1, ka * 8 + n0] = imag
    for ka in range(8):
        values = [(hold_ref[0, ka * 8 + n0], hold_ref[1, ka * 8 + n0]) for n0 in range(8)]
        for kb, value in enumerate(transform(values, sign)):
            store(ka + 8 * kb, value)


def middle_kernel(
    in_ref, shift_ref, mask_ref, forward_ref, inverse_ref, twiddle_ref, out_ref, mid_ref, back_ref, hold_ref
):
    for tile in range(2):
        sub = 8 * tile

        def load(s, sub=sub):
            return in_ref[s, sub : sub + 8, :], in_ref[s, 16 + sub : 24 + sub, :]

        def store(m1, value, sub=sub):
            real, imag = value
            tr, ti = twiddle_ref[0, m1 : m1 + 1, :], twiddle_ref[1, m1 : m1 + 1, :]
            at = m1 * 16 + sub
            mid_ref[at : at + 8, 0:128] = real * tr - imag * ti
            mid_ref[at : at + 8, 128:256] = real * ti + imag * tr

        column_transform(load, store, -1, hold_ref.at[0])
    forward, inverse = forward_ref[...], inverse_ref[...]
    for part in range(4):
        rows = slice(256 * part, 256 * part + 256)
        spectrum = matmul(spread(mid_ref[rows, :]), forward, ((1,), (0,)))
        real, imag = spectrum[:, :128], spectrum[:, 128:]
        for ref in range(2):
            cosine, sine = shift_ref[2 * ref, rows, :], shift_ref[2 * ref + 1, rows, :]
            turned = jnp.concatenate([real * cosine - imag * sine, real * sine + imag * cosine], axis=1)
            back_ref[ref, rows, :] = matmul(spread(turned), inverse, ((1,), (0,)))
    for tile in range(2):
        sub = 8 * tile
        for ref in range(2):

            def load(m1, ref=ref, sub=sub):
                at = m1 * 16 + sub
                real, imag = back_ref[ref, at : at + 8, 0:128], back_ref[ref, at : at + 8, 128:256]
                tr, ti = twiddle_ref[0, m1 : m1 + 1, :], twiddle_ref[1, m1 : m1 + 1, :]
                return real * tr + imag * ti, imag * tr - real * ti

            if ref == 0:

                def store(s, value, sub=sub):
                    out_ref[s, sub : sub + 8, :] = value[0]
                    out_ref[s, 16 + sub : 24 + sub, :] = value[1]

            else:

                def store(s, value, sub=sub):
                    chosen = mask_ref[s : s + 1, :] > 0.5
                    out_ref[s, sub : sub + 8, :] = jnp.where(chosen, value[0], out_ref[s, sub : sub + 8, :])
                    out_ref[s, 16 + sub : 24 + sub, :] = jnp.where(
                        chosen, value[1], out_ref[s, 16 + sub : 24 + sub, :]
                    )

            column_transform(load, store, 1, hold_ref.at[ref])


def inverse_y_kernel(in_ref, phase_ref, matrix_ref, twiddle_ref, out_ref, edge_ref, mid_ref):
    matrix = matrix_ref[...]
    for p in range(8):
        block = in_ref[8 * p : 8 * p + 8].reshape(256, 128)
        mid_ref[128 * p : 128 * p + 128, :] = matmul(spread(block.T), matrix, ((1,), (0,)))
    for field in range(2):
        for tile in range(4):
            rows = slice(8 * tile, 8 * tile + 8)
            values = []
            for k1 in range(NY_A):
                at = k1 * 64 + field * 32 + tile * 8
                real, imag = mid_ref[at : at + 8, 0:128], mid_ref[at : at + 8, 128:256]
                if k1:
                    tr, ti = twiddle_ref[0, k1 : k1 + 1, :], twiddle_ref[1, k1 : k1 + 1, :]
                    real, imag = real * tr + imag * ti, imag * tr - real * ti
                values.append((real, imag))
            for a, (real, imag) in enumerate(transform(values, 1)):
                lanes = slice(128 * a, 128 * a + 128)
                cosine, sine = phase_ref[0, rows, lanes], phase_ref[1, rows, lanes]
                if field == 0:
                    real, imag = real * cosine + imag * sine, imag * cosine - real * sine
                else:
                    real, imag = real * cosine - imag * sine, imag * cosine + real * sine
                for c, value in enumerate((real, imag)):
                    out_ref[field, c, rows, lanes] = value
                    row = 2 * field + c
                    if tile == 0:
                        edge_ref[0, row : row + 1, lanes] = value[0:1]
                    if tile == 3:
                        edge_ref[1, row : row + 1, lanes] = value[7:8]


def laplace_kernel(place_ref, wave_ref, above_ref, below_ref, coupling_ref, out_ref, *rest):
    image_refs, image_hold = rest[:4], rest[4]
    row = lax.broadcasted_iota(jnp.int32, (8, 2048), 0)
    lane = lax.broadcasted_iota(jnp.int32, (8, 2048), 1)
    for tile in range(4):
        rows = slice(8 * tile, 8 * tile + 8)
        coupling = coupling_ref[rows, :]
        results = []
        for field in range(2):
            laplace = []
            for c in range(2):
                value = wave_ref[field, c, rows, :]
                index = 2 * field + c
                if tile == 0:
                    before = above_ref[index : index + 1, :]
                else:
                    before = wave_ref[field, c, 8 * tile - 1 : 8 * tile, :]
                if tile == 3:
                    after = below_ref[index : index + 1, :]
                else:
                    after = wave_ref[field, c, 8 * tile + 8 : 8 * tile + 9, :]
                up = jnp.where(row == 0, before, pltpu.roll(value, 1, 0))
                down = jnp.where(row == 7, after, pltpu.roll(value, 7, 0))
                left = jnp.where(lane == 0, 0.0, pltpu.roll(value, 1, 1))
                right = jnp.where(lane == 2047, 0.0, pltpu.roll(value, 2047, 1))
                laplace.append(up + down + left + right - 4.0 * value)
            sign = -1.0 if field == 0 else 1.0
            scaled = coupling * sign
            real = wave_ref[field, 0, rows, :] - scaled * laplace[1]
            imag = wave_ref[field, 1, rows, :] + scaled * laplace[0]
            out_ref[field, 0, 0, rows, :] = real
            out_ref[field, 0, 1, rows, :] = imag
            results.append((real, imag))
        image_hold[rows, :] = results[0][0] * results[1][0] + results[0][1] * results[1][1]
    place = place_ref[0]
    for k in range(4):
        at = pl.multiple_of(((place + k) % 4) * 8, 8)
        image_refs[k][...] = image_hold[pl.ds(at, 8), :]


def assemble_kernel(place_ref, own_ref, *rest):
    others, out_ref = rest[:3], rest[3]
    place = place_ref[0]
    for k, ref in enumerate((own_ref,) + tuple(others)):
        at = pl.multiple_of(((place + 4 - k) % 4) * 8, 8)
        out_ref[0, pl.ds(at, 8), :] = ref[...]


def whole(memory=pltpu.VMEM):
    return pl.BlockSpec(memory_space=memory)


def f32(*shape):
    return jax.ShapeDtypeStruct(shape, jnp.float32)


def call(kernel, out_shape, operands, scratch=(), smem=0, near=(), near_out=False):
    many = isinstance(out_shape, (tuple, list))
    if not INTERPRET:
        operands = tuple(
            pltpu.with_memory_space_constraint(x, pltpu.VMEM) if i in near else x
            for i, x in enumerate(operands)
        )
        if near_out:
            shapes = out_shape if many else (out_shape,)
            shapes = tuple(pltpu.VMEM(x.shape, x.dtype) for x in shapes)
            out_shape = shapes if many else shapes[0]
    return pl.pallas_call(
        kernel,
        out_shape=out_shape,
        in_specs=[whole(pltpu.SMEM)] * smem + [whole()] * (len(operands) - smem),
        out_specs=[whole()] * len(out_shape) if many else whole(),
        scratch_shapes=list(scratch),
        interpret=INTERPRET,
        compiler_params=pltpu.CompilerParams(vmem_limit_bytes=VMEM_BYTES),
    )(*operands)


def forward_y(wavefields):
    const = constants()
    return call(
        forward_y_kernel,
        f32(64, 32, 128),
        (wavefields, jnp.asarray(const["y_forward"]), jnp.asarray(const["y_twiddle"])),
        (pltpu.VMEM((1024, 256), jnp.float32),),
        near_out=True,
    )


def middle(blocks, shift, mask):
    const = constants()
    return call(
        middle_kernel,
        f32(64, 32, 128),
        (
            blocks,
            shift,
            mask,
            jnp.asarray(const["x_forward"]),
            jnp.asarray(const["x_inverse"]),
            jnp.asarray(const["x_twiddle"]),
        ),
        (
            pltpu.VMEM((1024, 256), jnp.float32),
            pltpu.VMEM((2, 1024, 256), jnp.float32),
            pltpu.VMEM((2, 2, 64, 8, 128), jnp.float32),
        ),
        near=(0, 1, 2),
        near_out=True,
    )


def inverse_y(blocks, phase):
    const = constants()
    return call(
        inverse_y_kernel,
        (f32(2, 2, 32, 2048), f32(2, 4, 2048)),
        (blocks, phase, jnp.asarray(const["y_inverse"]), jnp.asarray(const["y_twiddle"])),
        (pltpu.VMEM((1024, 256), jnp.float32),),
        near=(0, 1),
        near_out=True,
    )


def laplace(place, wave, above, below, coupling):
    return call(
        laplace_kernel,
        (f32(2, 1, 2, 32, 2048),) + (f32(8, 2048),) * 4,
        (place, wave, above, below, coupling),
        (pltpu.VMEM((32, 2048), jnp.float32),),
        smem=1,
    )


def assemble(place, pieces):
    return call(assemble_kernel, f32(1, 32, 2048), (place,) + tuple(pieces), smem=1)


def wave_values(number, length):
    signed = jnp.where(number < length // 2, number, number - length)
    return 2.0 * math.pi / length * signed.astype(jnp.float32)


def shift_tables(space_index, omega, ref_velocity):
    row = lax.broadcasted_iota(jnp.int32, (1024, 128), 0)
    lane = lax.broadcasted_iota(jnp.int32, (1024, 128), 1)
    kx = wave_values(row // 16 + 64 * (lane % 32), NX)
    k1 = 2 * (space_index // 8) + lane // 64
    k2 = 16 * (space_index % 8) + row % 16
    ky = wave_values(k1 + 16 * k2, NY)
    sign = jnp.where((lane // 32) % 2 == 0, -1.0, 1.0).astype(jnp.float32)
    squared = kx**2 + ky**2
    tables = []
    for ref in range(2):
        vertical = (omega / ref_velocity[ref]) ** 2 - squared
        root = DZ * jnp.sqrt(jnp.abs(vertical))
        travels = vertical >= 0.0
        tables.append(jnp.where(travels, jnp.cos(root), jnp.exp(-root)))
        tables.append(jnp.where(travels, sign * jnp.sin(root), 0.0))
    return jnp.stack(tables)


def mask_table(ref_index):
    return jnp.tile(jnp.repeat(ref_index.reshape(64, 2), 16, axis=1), (1, 4)).astype(jnp.float32)


def phase_tables(speed, ref_rows, omega):
    time_shift = omega * DZ * (1.0 / speed - 1.0 / ref_rows)
    return jnp.stack([jnp.cos(time_shift), jnp.sin(time_shift)])


def coupling_table(speed, ref_rows, omega):
    return DZ * (speed - ref_rows) * ref_rows / (16.0 * omega)


def shifted_pairs(step, count=4):
    return [(i, (i + step) % count) for i in range(count)]


def slab_speed(velocity, owner, freq_index):
    stored = lax.dynamic_index_in_dim(velocity, owner % 4, 0, keepdims=False).reshape(4, 8, 2048)
    source = owner // 4
    mine = lax.dynamic_index_in_dim(stored, freq_index, 0, keepdims=False)
    for step in (1, 2, 3):
        piece = lax.dynamic_index_in_dim(stored, (freq_index + step) % 4, 0, keepdims=False)
        arrived = lax.ppermute(piece, "freq", shifted_pairs(step))
        mine = jnp.where((freq_index + 4 - step) % 4 == source, arrived, mine)
    return gathered(mine)


def gathered(mine):
    return [mine] + [lax.ppermute(mine, "freq", shifted_pairs(step)) for step in (1, 2, 3)]


def per_device(wavefields, frequencies, velocity, slab_owner, ref_velocity, ref_index):
    space_index = lax.axis_index("space")
    freq_index = lax.axis_index("freq")
    place = freq_index.reshape(1).astype(jnp.int32)
    omega = frequencies[0]
    blocks = forward_y(wavefields)
    blocks = lax.all_to_all(blocks, "space", split_axis=0, concat_axis=0, tiled=True)
    shift = shift_tables(space_index, omega, ref_velocity[0])
    speed = assemble(place, slab_speed(velocity, slab_owner[0], freq_index))[0]
    local_refs = lax.dynamic_slice_in_dim(ref_index[0], 2 * space_index, 2)
    ref_rows = jnp.repeat(ref_velocity[0][local_refs], 16)[:, None]
    phase = phase_tables(speed, ref_rows, omega)
    coupling = coupling_table(speed, ref_rows, omega)
    mask = mask_table(ref_index[0])
    blocks, shift, mask, phase, coupling = lax.optimization_barrier((blocks, shift, mask, phase, coupling))
    blocks = middle(blocks, shift, mask)
    blocks = lax.all_to_all(blocks, "space", split_axis=0, concat_axis=0, tiled=True)
    wave, edges = inverse_y(blocks, phase)
    count = 64
    above = lax.ppermute(edges[1], "space", [(i, i + 1) for i in range(count - 1)])
    below = lax.ppermute(edges[0], "space", [(i + 1, i) for i in range(count - 1)])
    fields, *quarters = laplace(place, wave, above, below, coupling)
    total = quarters[0]
    for step in (1, 2, 3):
        total = total + lax.ppermute(quarters[step], "freq", shifted_pairs(step))
    image = assemble(place, gathered(total))
    return fields, image


def solution(mesh):
    in_specs = (
        P(None, "freq", None, "space", None),
        P("freq"),
        P("freq", "space", None),
        P(),
        P(),
        P(),
    )
    out_specs = (P(None, "freq", None, "space", None), P(None, "space", None))
    return jax.shard_map(
        per_device, mesh=mesh, in_specs=in_specs, out_specs=out_specs, check_vma=False
    )
```

```python
import functools
import math

import jax
import jax.numpy as jnp
import numpy as np
from jax import lax
from jax.experimental import pallas as pl
from jax.experimental.pallas import tpu as pltpu
from jax.sharding import PartitionSpec as P


DZ = 4
INTERPRET = False
VMEM_BYTES = 20 * 2**20
BF16 = jnp.bfloat16

NY_A, NY_B = 16, 128
NX_S, NX_R = 64, 32
NY, NX = NY_A * NY_B, NX_S * NX_R


def split_bf16(matrix):
    high = np.asarray(matrix, np.float32).astype(BF16)
    low = (np.asarray(matrix, np.float64) - high.astype(np.float64)).astype(np.float32).astype(BF16)
    return high, low


@functools.cache
def constants():
    k2 = np.arange(NY_B)
    b = np.arange(NY_B)
    angle = 2.0 * np.pi * (np.outer(k2, b) % NY_B) / NY_B
    cosine, sine = np.cos(angle), np.sin(angle)
    forward = np.stack(
        [np.concatenate([cosine, sine], 1), np.concatenate([-sine, cosine], 1)], 0
    )
    forward = forward.reshape(2, 8, 16, 256).transpose(1, 0, 2, 3).reshape(256, 256)
    inverse = forward.copy() / NY
    fh, fl = split_bf16(forward)
    y_forward = np.concatenate([fh, fl, fh], 1)
    ih, il = split_bf16(inverse)
    y_inverse = np.concatenate([ih, il, ih], 0)
    r = np.arange(NX_R)
    angle = 2.0 * np.pi * (np.outer(r, r) % NX_R) / NX_R
    cosine = np.kron(np.eye(4), np.cos(angle))
    sine = np.kron(np.eye(4), np.sin(angle))
    x_forward = np.block([[cosine, -sine], [sine, cosine]])
    x_inverse = np.block([[cosine, sine], [-sine, cosine]]) / NX
    xh, xl = split_bf16(x_forward)
    x_forward = np.concatenate([xh, xl, xh], 0)
    xh, xl = split_bf16(x_inverse)
    x_inverse = np.concatenate([xh, xl, xh], 0)
    angle = 2.0 * np.pi * np.outer(np.arange(NY_A), b) / NY
    y_twiddle = np.stack([np.cos(angle), -np.sin(angle)]).astype(np.float32)
    angle = 2.0 * np.pi * np.outer(np.arange(NX_S), np.tile(r, 4)) / NX
    x_twiddle = np.stack([np.cos(angle), -np.sin(angle)]).astype(np.float32)
    return dict(
        y_forward=y_forward,
        y_inverse=y_inverse,
        x_forward=x_forward,
        x_inverse=x_inverse,
        y_twiddle=y_twiddle,
        x_twiddle=x_twiddle,
    )


def times(value, numerator, length, sign):
    real, imag = value
    turn = (sign * numerator) % length
    eighth = turn * 8
    if turn == 0:
        return real, imag
    if eighth % length == 0:
        step = eighth // length
        half = math.sqrt(0.5)
        if step == 2:
            return -imag, real
        if step == 4:
            return -real, -imag
        if step == 6:
            return imag, -real
        if step == 1:
            return (real - imag) * half, (real + imag) * half
        if step == 3:
            return (real + imag) * -half, (real - imag) * half
        if step == 5:
            return (imag - real) * half, (real + imag) * -half
        return (real + imag) * half, (imag - real) * half
    cosine = math.cos(2.0 * math.pi * turn / length)
    sine = math.sin(2.0 * math.pi * turn / length)
    return real * cosine - imag * sine, real * sine + imag * cosine


def plus(left, right):
    return left[0] + right[0], left[1] + right[1]


def minus(left, right):
    return left[0] - right[0], left[1] - right[1]


def transform(values, sign):
    length = len(values)
    if length == 1:
        return values
    if length == 2:
        return [plus(values[0], values[1]), minus(values[0], values[1])]
    if length == 4:
        even_sum, even_diff = plus(values[0], values[2]), minus(values[0], values[2])
        odd_sum, odd_diff = plus(values[1], values[3]), minus(values[1], values[3])
        if sign > 0:
            first = (even_diff[0] - odd_diff[1], even_diff[1] + odd_diff[0])
            third = (even_diff[0] + odd_diff[1], even_diff[1] - odd_diff[0])
        else:
            first = (even_diff[0] + odd_diff[1], even_diff[1] - odd_diff[0])
            third = (even_diff[0] - odd_diff[1], even_diff[1] + odd_diff[0])
        return [plus(even_sum, odd_sum), first, minus(even_sum, odd_sum), third]
    radix = 4 if length % 4 == 0 and length > 8 else 2
    rest = length // radix
    columns = [transform(values[i::radix], sign) for i in range(radix)]
    result = [None] * length
    for k in range(rest):
        picked = [times(columns[i][k], i * k, length, sign) for i in range(radix)]
        for q, value in enumerate(transform(picked, sign)):
            result[k + rest * q] = value
    return result


def spread(value):
    high = value.astype(BF16)
    low = (value - high.astype(jnp.float32)).astype(BF16)
    return jnp.concatenate([high, high, low], axis=1)


def matmul(left, right, contract):
    return lax.dot_general(left, right, (contract, ((), ())), preferred_element_type=jnp.float32)


def fetch(sources, targets, sems):
    copies = [pltpu.make_async_copy(s, t, sems.at[i]) for i, (s, t) in enumerate(zip(sources, targets))]
    for copy in copies:
        copy.start()
    return copies


def forward_y_kernel(wave_hbm, matrix_hbm, twiddle_hbm, out_ref, wave_ref, matrix_ref, twiddle_ref, mid_ref, sems):
    parts = [(field, slice(8 * tile, 8 * tile + 8)) for field in range(2) for tile in range(4)]
    views = [[ref.at[field, 0, :, rows, :] for field, rows in parts] for ref in (wave_hbm, wave_ref)]
    waits = fetch([twiddle_hbm] + views[0] + [matrix_hbm], [twiddle_ref] + views[1] + [matrix_ref], sems)
    waits[0].wait()
    for field in range(2):
        for tile in range(4):
            waits[1 + 4 * field + tile].wait()
            rows = slice(8 * tile, 8 * tile + 8)
            values = [
                tuple(wave_ref[field, 0, c, rows, 128 * a : 128 * a + 128] for c in range(2))
                for a in range(NY_A)
            ]
            for k1, (real, imag) in enumerate(transform(values, -1)):
                if k1:
                    tr, ti = twiddle_ref[0, k1 : k1 + 1, :], twiddle_ref[1, k1 : k1 + 1, :]
                    real, imag = real * tr - imag * ti, real * ti + imag * tr
                at = k1 * 64 + field * 32 + tile * 8
                mid_ref[at : at + 8, 0:128] = real
                mid_ref[at : at + 8, 128:256] = imag
    waits[9].wait()
    matrix = matrix_ref[...]
    for pair in range(4):
        packed = spread(mid_ref[256 * pair : 256 * pair + 256, :])
        product = matmul(matrix, packed, ((1,), (1,)))
        for half in range(2):
            at = 16 * pair + 8 * half
            out_ref[at : at + 8] = product[:, 128 * half : 128 * half + 128].reshape(8, 32, 128)


def column_transform(load, store, sign, hold_ref):
    for n0 in range(8):
        piece = transform([load(8 * n1 + n0) for n1 in range(8)], sign)
        for ka in range(8):
            real, imag = times(piece[ka], n0 * ka, 64, sign)
            hold_ref[0, ka * 8 + n0] = real
            hold_ref[1, ka * 8 + n0] = imag
    for ka in range(8):
        values = [(hold_ref[0, ka * 8 + n0], hold_ref[1, ka * 8 + n0]) for n0 in range(8)]
        for kb, value in enumerate(transform(values, sign)):
            store(ka + 8 * kb, value)


def middle_kernel(
    refs_ref,
    in_ref,
    shift_ref,
    forward_hbm,
    inverse_hbm,
    twiddle_hbm,
    out_ref,
    forward_ref,
    inverse_ref,
    twiddle_ref,
    mid_ref,
    back_ref,
    hold_ref,
    sems,
):
    waits = fetch(
        [twiddle_hbm, forward_hbm, inverse_hbm], [twiddle_ref, forward_ref, inverse_ref], sems
    )
    waits[0].wait()
    early = lax.broadcasted_iota(jnp.int32, (8, 128), 1) % 32 < 16
    for tile in range(2):
        sub = 8 * tile

        def load(s, sub=sub):
            return in_ref[s, sub : sub + 8, :], in_ref[s, 16 + sub : 24 + sub, :]

        def store(m1, value, sub=sub):
            real, imag = value
            tr, ti = twiddle_ref[0, m1 : m1 + 1, :], twiddle_ref[1, m1 : m1 + 1, :]
            at = m1 * 16 + sub
            mid_ref[at : at + 8, 0:128] = real * tr - imag * ti
            mid_ref[at : at + 8, 128:256] = real * ti + imag * tr

        column_transform(load, store, -1, hold_ref.at[0])
    waits[1].wait()
    waits[2].wait()
    forward, inverse = forward_ref[...], inverse_ref[...]
    for part in range(4):
        rows = slice(256 * part, 256 * part + 256)
        spectrum = matmul(spread(mid_ref[rows, :]), forward, ((1,), (0,)))
        real, imag = spectrum[:, :128], spectrum[:, 128:]
        for ref in range(2):
            cosine, sine = shift_ref[2 * ref, rows, :], shift_ref[2 * ref + 1, rows, :]
            turned = jnp.concatenate([real * cosine - imag * sine, real * sine + imag * cosine], axis=1)
            back_ref[ref, rows, :] = matmul(spread(turned), inverse, ((1,), (0,)))
    for tile in range(2):
        sub = 8 * tile
        for ref in range(2):

            def load(m1, ref=ref, sub=sub):
                at = m1 * 16 + sub
                real, imag = back_ref[ref, at : at + 8, 0:128], back_ref[ref, at : at + 8, 128:256]
                tr, ti = twiddle_ref[0, m1 : m1 + 1, :], twiddle_ref[1, m1 : m1 + 1, :]
                return real * tr + imag * ti, imag * tr - real * ti

            if ref == 0:

                def store(s, value, sub=sub):
                    out_ref[s, sub : sub + 8, :] = value[0]
                    out_ref[s, 16 + sub : 24 + sub, :] = value[1]

            else:

                def store(s, value, sub=sub):
                    chosen = jnp.where(early, refs_ref[0, 2 * s], refs_ref[0, 2 * s + 1]) > 0
                    out_ref[s, sub : sub + 8, :] = jnp.where(chosen, value[0], out_ref[s, sub : sub + 8, :])
                    out_ref[s, 16 + sub : 24 + sub, :] = jnp.where(
                        chosen, value[1], out_ref[s, 16 + sub : 24 + sub, :]
                    )

            column_transform(load, store, 1, hold_ref.at[ref])


def inverse_y_kernel(in_ref, phase_ref, matrix_ref, twiddle_ref, out_ref, edge_ref, mid_ref):
    matrix = matrix_ref[...]
    for p in range(8):
        block = in_ref[8 * p : 8 * p + 8].reshape(256, 128)
        mid_ref[128 * p : 128 * p + 128, :] = matmul(spread(block.T), matrix, ((1,), (0,)))
    for field in range(2):
        for tile in range(4):
            rows = slice(8 * tile, 8 * tile + 8)
            values = []
            for k1 in range(NY_A):
                at = k1 * 64 + field * 32 + tile * 8
                real, imag = mid_ref[at : at + 8, 0:128], mid_ref[at : at + 8, 128:256]
                if k1:
                    tr, ti = twiddle_ref[0, k1 : k1 + 1, :], twiddle_ref[1, k1 : k1 + 1, :]
                    real, imag = real * tr + imag * ti, imag * tr - real * ti
                values.append((real, imag))
            for a, (real, imag) in enumerate(transform(values, 1)):
                lanes = slice(128 * a, 128 * a + 128)
                cosine, sine = phase_ref[0, rows, lanes], phase_ref[1, rows, lanes]
                if field == 0:
                    real, imag = real * cosine + imag * sine, imag * cosine - real * sine
                else:
                    real, imag = real * cosine - imag * sine, imag * cosine + real * sine
                for c, value in enumerate((real, imag)):
                    out_ref[field, c, rows, lanes] = value
                    row = 2 * field + c
                    if tile == 0:
                        edge_ref[0, row : row + 1, lanes] = value[0:1]
                    if tile == 3:
                        edge_ref[1, row : row + 1, lanes] = value[7:8]


def laplace_kernel(place_ref, wave_ref, above_ref, below_ref, coupling_ref, out_ref, *rest):
    image_refs, image_hold = rest[:4], rest[4]
    row = lax.broadcasted_iota(jnp.int32, (8, 2048), 0)
    lane = lax.broadcasted_iota(jnp.int32, (8, 2048), 1)
    for tile in range(4):
        rows = slice(8 * tile, 8 * tile + 8)
        coupling = coupling_ref[rows, :]
        results = []
        for field in range(2):
            laplace = []
            for c in range(2):
                value = wave_ref[field, c, rows, :]
                index = 2 * field + c
                if tile == 0:
                    before = above_ref[index : index + 1, :]
                else:
                    before = wave_ref[field, c, 8 * tile - 1 : 8 * tile, :]
                if tile == 3:
                    after = below_ref[index : index + 1, :]
                else:
                    after = wave_ref[field, c, 8 * tile + 8 : 8 * tile + 9, :]
                up = jnp.where(row == 0, before, pltpu.roll(value, 1, 0))
                down = jnp.where(row == 7, after, pltpu.roll(value, 7, 0))
                left = jnp.where(lane == 0, 0.0, pltpu.roll(value, 1, 1))
                right = jnp.where(lane == 2047, 0.0, pltpu.roll(value, 2047, 1))
                laplace.append(up + down + left + right - 4.0 * value)
            sign = -1.0 if field == 0 else 1.0
            scaled = coupling * sign
            real = wave_ref[field, 0, rows, :] - scaled * laplace[1]
            imag = wave_ref[field, 1, rows, :] + scaled * laplace[0]
            out_ref[field, 0, 0, rows, :] = real
            out_ref[field, 0, 1, rows, :] = imag
            results.append((real, imag))
        image_hold[rows, :] = results[0][0] * results[1][0] + results[0][1] * results[1][1]
    place = place_ref[0]
    for k in range(4):
        at = pl.multiple_of(((place + k) % 4) * 8, 8)
        image_refs[k][...] = image_hold[pl.ds(at, 8), :]


def assemble_kernel(place_ref, own_ref, *rest):
    others, out_ref = rest[:3], rest[3]
    place = place_ref[0]
    for k, ref in enumerate((own_ref,) + tuple(others)):
        at = pl.multiple_of(((place + 4 - k) % 4) * 8, 8)
        out_ref[0, pl.ds(at, 8), :] = ref[...]


def whole(memory=pltpu.VMEM):
    return pl.BlockSpec(memory_space=memory)


def f32(*shape):
    return jax.ShapeDtypeStruct(shape, jnp.float32)


def call(kernel, out_shape, operands, scratch=(), smem=0, far=0, near=(), near_out=False):
    many = isinstance(out_shape, (tuple, list))
    if not INTERPRET:
        operands = tuple(
            pltpu.with_memory_space_constraint(x, pltpu.VMEM)
            if i in near
            else pltpu.with_memory_space_constraint(x, pltpu.HBM) if i >= len(operands) - far else x
            for i, x in enumerate(operands)
        )
        if near_out:
            shapes = out_shape if many else (out_shape,)
            shapes = tuple(pltpu.VMEM(x.shape, x.dtype) for x in shapes)
            out_shape = shapes if many else shapes[0]
    return pl.pallas_call(
        kernel,
        out_shape=out_shape,
        in_specs=[whole(pltpu.SMEM)] * smem
        + [whole()] * (len(operands) - smem - far)
        + [whole(pl.ANY if INTERPRET else pltpu.HBM)] * far,
        out_specs=[whole()] * len(out_shape) if many else whole(),
        scratch_shapes=list(scratch),
        interpret=INTERPRET,
        compiler_params=pltpu.CompilerParams(vmem_limit_bytes=VMEM_BYTES),
    )(*operands)


def forward_y(wavefields):
    const = constants()
    return call(
        forward_y_kernel,
        f32(64, 32, 128),
        (wavefields, jnp.asarray(const["y_forward"]), jnp.asarray(const["y_twiddle"])),
        (
            pltpu.VMEM((2, 1, 2, 32, 2048), jnp.float32),
            pltpu.VMEM((256, 768), BF16),
            pltpu.VMEM((2, 16, 128), jnp.float32),
            pltpu.VMEM((1024, 256), jnp.float32),
            pltpu.SemaphoreType.DMA((10,)),
        ),
        far=3,
        near_out=True,
    )


def middle(blocks, shift, ref_index):
    const = constants()
    return call(
        middle_kernel,
        f32(64, 32, 128),
        (
            ref_index,
            blocks,
            shift,
            jnp.asarray(const["x_forward"]),
            jnp.asarray(const["x_inverse"]),
            jnp.asarray(const["x_twiddle"]),
        ),
        (
            pltpu.VMEM((768, 256), BF16),
            pltpu.VMEM((768, 256), BF16),
            pltpu.VMEM((2, 64, 128), jnp.float32),
            pltpu.VMEM((1024, 256), jnp.float32),
            pltpu.VMEM((2, 1024, 256), jnp.float32),
            pltpu.VMEM((2, 2, 64, 8, 128), jnp.float32),
            pltpu.SemaphoreType.DMA((3,)),
        ),
        smem=1,
        far=3,
        near=(1, 2),
        near_out=True,
    )


def inverse_y(blocks, phase):
    const = constants()
    return call(
        inverse_y_kernel,
        (f32(2, 2, 32, 2048), f32(2, 4, 2048)),
        (blocks, phase, jnp.asarray(const["y_inverse"]), jnp.asarray(const["y_twiddle"])),
        (pltpu.VMEM((1024, 256), jnp.float32),),
        near=(0, 1),
        near_out=True,
    )


def laplace(place, wave, above, below, coupling):
    return call(
        laplace_kernel,
        (f32(2, 1, 2, 32, 2048),) + (f32(8, 2048),) * 4,
        (place, wave, above, below, coupling),
        (pltpu.VMEM((32, 2048), jnp.float32),),
        smem=1,
    )


def assemble(place, pieces):
    return call(assemble_kernel, f32(1, 32, 2048), (place,) + tuple(pieces), smem=1)


def wave_values(number, length):
    signed = jnp.where(number < length // 2, number, number - length)
    return 2.0 * math.pi / length * signed.astype(jnp.float32)


def shift_tables(space_index, omega, ref_velocity):
    row = lax.broadcasted_iota(jnp.int32, (1024, 128), 0)
    lane = lax.broadcasted_iota(jnp.int32, (1024, 128), 1)
    kx = wave_values(row // 16 + 64 * (lane % 32), NX)
    k1 = 2 * (space_index // 8) + lane // 64
    k2 = 16 * (space_index % 8) + row % 16
    ky = wave_values(k1 + 16 * k2, NY)
    sign = jnp.where((lane // 32) % 2 == 0, -1.0, 1.0).astype(jnp.float32)
    squared = kx**2 + ky**2
    tables = []
    for ref in range(2):
        vertical = (omega / ref_velocity[ref]) ** 2 - squared
        root = DZ * jnp.sqrt(jnp.abs(vertical))
        travels = vertical >= 0.0
        tables.append(jnp.where(travels, jnp.cos(root), jnp.exp(-root)))
        tables.append(jnp.where(travels, sign * jnp.sin(root), 0.0))
    return jnp.stack(tables)


def phase_tables(speed, ref_rows, omega):
    time_shift = omega * DZ * (1.0 / speed - 1.0 / ref_rows)
    return jnp.stack([jnp.cos(time_shift), jnp.sin(time_shift)])


def coupling_table(speed, ref_rows, omega):
    return DZ * (speed - ref_rows) * ref_rows / (16.0 * omega)


def shifted_pairs(step, count=4):
    return [(i, (i + step) % count) for i in range(count)]


def slab_speed(velocity, owner, freq_index):
    stored = lax.dynamic_index_in_dim(velocity, owner % 4, 0, keepdims=False).reshape(4, 8, 2048)
    source = owner // 4
    mine = lax.dynamic_index_in_dim(stored, freq_index, 0, keepdims=False)
    for step in (1, 2, 3):
        piece = lax.dynamic_index_in_dim(stored, (freq_index + step) % 4, 0, keepdims=False)
        arrived = lax.ppermute(piece, "freq", shifted_pairs(step))
        mine = jnp.where((freq_index + 4 - step) % 4 == source, arrived, mine)
    return gathered(mine)


def gathered(mine):
    pieces = [mine]
    for step in (1, 2, 3):
        pieces.append(lax.ppermute(mine, "freq", shifted_pairs(step)))
    return pieces


def exchange(blocks):
    return lax.all_to_all(blocks, "space", split_axis=0, concat_axis=0, tiled=True)


def step_down(wavefields, frequencies, velocity, slab_owner, ref_velocity, ref_index):
    space_index = lax.axis_index("space")
    freq_index = lax.axis_index("freq")
    place = freq_index.reshape(1).astype(jnp.int32)
    omega = frequencies[0]
    slab = slab_speed(velocity, slab_owner[0], freq_index)
    blocks = forward_y(wavefields)
    blocks = exchange(blocks)
    shift = shift_tables(space_index, omega, ref_velocity[0])
    speed = assemble(place, slab)[0]
    local_refs = lax.dynamic_slice_in_dim(ref_index[0], 2 * space_index, 2)
    ref_rows = jnp.repeat(ref_velocity[0][local_refs], 16)[:, None]
    phase = phase_tables(speed, ref_rows, omega)
    coupling = coupling_table(speed, ref_rows, omega)
    blocks = middle(blocks, shift, ref_index)
    blocks = exchange(blocks)
    wave, edges = inverse_y(blocks, phase)
    count = 64
    above = lax.ppermute(edges[1], "space", [(i, i + 1) for i in range(count - 1)])
    below = lax.ppermute(edges[0], "space", [(i + 1, i) for i in range(count - 1)])
    fields, *quarters = laplace(place, wave, above, below, coupling)
    total = quarters[0]
    for step in (1, 2, 3):
        total = total + lax.ppermute(quarters[step], "freq", shifted_pairs(step))
    image = assemble(place, gathered(total))
    return fields, image


def solution(mesh):
    in_specs = (
        P(None, "freq", None, "space", None),
        P("freq"),
        P("freq", "space", None),
        P(),
        P(),
        P(),
    )
    out_specs = (P(None, "freq", None, "space", None), P(None, "space", None))
    return jax.shard_map(
        step_down, mesh=mesh, in_specs=in_specs, out_specs=out_specs, check_vma=False
    )
```

```python
import functools
import math

import jax
import jax.numpy as jnp
import numpy as np
from jax import lax
from jax.experimental import pallas as pl
from jax.experimental.pallas import tpu as pltpu
from jax.sharding import PartitionSpec as P


DZ = 4
INTERPRET = False
VMEM_BYTES = 20 * 2**20
BF16 = jnp.bfloat16

NY_A, NY_B = 16, 128
NX_S, NX_R = 64, 32
NY, NX = NY_A * NY_B, NX_S * NX_R


def split_bf16(matrix):
    high = np.asarray(matrix, np.float32).astype(BF16)
    low = (np.asarray(matrix, np.float64) - high.astype(np.float64)).astype(np.float32).astype(BF16)
    return high, low


@functools.cache
def constants():
    k2 = np.arange(NY_B)
    b = np.arange(NY_B)
    angle = 2.0 * np.pi * (np.outer(k2, b) % NY_B) / NY_B
    cosine, sine = np.cos(angle), np.sin(angle)
    forward = np.stack(
        [np.concatenate([cosine, sine], 1), np.concatenate([-sine, cosine], 1)], 0
    )
    forward = forward.reshape(2, 8, 16, 256).transpose(1, 0, 2, 3).reshape(256, 256)
    inverse = forward.copy() / NY
    fh, fl = split_bf16(forward)
    y_forward = np.concatenate([fh, fl, fh], 1)
    ih, il = split_bf16(inverse)
    y_inverse = np.concatenate([ih, il, ih], 0)
    r = np.arange(NX_R)
    angle = 2.0 * np.pi * (np.outer(r, r) % NX_R) / NX_R
    cosine = np.kron(np.eye(4), np.cos(angle))
    sine = np.kron(np.eye(4), np.sin(angle))
    x_forward = np.block([[cosine, -sine], [sine, cosine]])
    x_inverse = np.block([[cosine, sine], [-sine, cosine]]) / NX
    xh, xl = split_bf16(x_forward)
    x_forward = np.concatenate([xh, xl, xh], 0)
    xh, xl = split_bf16(x_inverse)
    x_inverse = np.concatenate([xh, xl, xh], 0)
    angle = 2.0 * np.pi * np.outer(np.arange(NY_A), b) / NY
    y_twiddle = np.stack([np.cos(angle), -np.sin(angle)]).astype(np.float32)
    angle = 2.0 * np.pi * np.outer(np.arange(NX_S), np.tile(r, 4)) / NX
    x_twiddle = np.stack([np.cos(angle), -np.sin(angle)]).astype(np.float32)
    return dict(
        y_forward=y_forward,
        y_inverse=y_inverse,
        x_forward=x_forward,
        x_inverse=x_inverse,
        y_twiddle=y_twiddle,
        x_twiddle=x_twiddle,
    )


def times(value, numerator, length, sign):
    real, imag = value
    turn = (sign * numerator) % length
    eighth = turn * 8
    if turn == 0:
        return real, imag
    if eighth % length == 0:
        step = eighth // length
        half = math.sqrt(0.5)
        if step == 2:
            return -imag, real
        if step == 4:
            return -real, -imag
        if step == 6:
            return imag, -real
        if step == 1:
            return (real - imag) * half, (real + imag) * half
        if step == 3:
            return (real + imag) * -half, (real - imag) * half
        if step == 5:
            return (imag - real) * half, (real + imag) * -half
        return (real + imag) * half, (imag - real) * half
    cosine = math.cos(2.0 * math.pi * turn / length)
    sine = math.sin(2.0 * math.pi * turn / length)
    return real * cosine - imag * sine, real * sine + imag * cosine


def plus(left, right):
    return left[0] + right[0], left[1] + right[1]


def minus(left, right):
    return left[0] - right[0], left[1] - right[1]


def transform(values, sign):
    length = len(values)
    if length == 1:
        return values
    if length == 2:
        return [plus(values[0], values[1]), minus(values[0], values[1])]
    if length == 4:
        even_sum, even_diff = plus(values[0], values[2]), minus(values[0], values[2])
        odd_sum, odd_diff = plus(values[1], values[3]), minus(values[1], values[3])
        if sign > 0:
            first = (even_diff[0] - odd_diff[1], even_diff[1] + odd_diff[0])
            third = (even_diff[0] + odd_diff[1], even_diff[1] - odd_diff[0])
        else:
            first = (even_diff[0] + odd_diff[1], even_diff[1] - odd_diff[0])
            third = (even_diff[0] - odd_diff[1], even_diff[1] + odd_diff[0])
        return [plus(even_sum, odd_sum), first, minus(even_sum, odd_sum), third]
    radix = 4 if length % 4 == 0 and length > 8 else 2
    rest = length // radix
    columns = [transform(values[i::radix], sign) for i in range(radix)]
    result = [None] * length
    for k in range(rest):
        picked = [times(columns[i][k], i * k, length, sign) for i in range(radix)]
        for q, value in enumerate(transform(picked, sign)):
            result[k + rest * q] = value
    return result


def spread(value):
    high = value.astype(BF16)
    low = (value - high.astype(jnp.float32)).astype(BF16)
    return jnp.concatenate([high, high, low], axis=1)


def matmul(left, right, contract):
    return lax.dot_general(left, right, (contract, ((), ())), preferred_element_type=jnp.float32)


def fetch(sources, targets, sems):
    copies = [pltpu.make_async_copy(s, t, sems.at[i]) for i, (s, t) in enumerate(zip(sources, targets))]
    for copy in copies:
        copy.start()
    return copies


def forward_y_kernel(wave_hbm, matrix_hbm, twiddle_hbm, out_ref, wave_ref, matrix_ref, twiddle_ref, mid_ref, sems):
    parts = [(field, slice(8 * tile, 8 * tile + 8)) for field in range(2) for tile in range(4)]
    views = [[ref.at[field, 0, :, rows, :] for field, rows in parts] for ref in (wave_hbm, wave_ref)]
    waits = fetch([twiddle_hbm] + views[0] + [matrix_hbm], [twiddle_ref] + views[1] + [matrix_ref], sems)
    waits[0].wait()
    for field in range(2):
        for tile in range(4):
            waits[1 + 4 * field + tile].wait()
            rows = slice(8 * tile, 8 * tile + 8)
            values = [
                tuple(wave_ref[field, 0, c, rows, 128 * a : 128 * a + 128] for c in range(2))
                for a in range(NY_A)
            ]
            for k1, (real, imag) in enumerate(transform(values, -1)):
                if k1:
                    tr, ti = twiddle_ref[0, k1 : k1 + 1, :], twiddle_ref[1, k1 : k1 + 1, :]
                    real, imag = real * tr - imag * ti, real * ti + imag * tr
                at = k1 * 64 + field * 32 + tile * 8
                mid_ref[at : at + 8, 0:128] = real
                mid_ref[at : at + 8, 128:256] = imag
    waits[9].wait()
    matrix = matrix_ref[...]
    for pair in range(4):
        packed = spread(mid_ref[256 * pair : 256 * pair + 256, :])
        product = matmul(matrix, packed, ((1,), (1,)))
        for half in range(2):
            at = 16 * pair + 8 * half
            out_ref[at : at + 8] = product[:, 128 * half : 128 * half + 128].reshape(8, 32, 128)


def column_transform(load, store, sign, hold_ref):
    for n0 in range(8):
        piece = transform([load(8 * n1 + n0) for n1 in range(8)], sign)
        for ka in range(8):
            real, imag = times(piece[ka], n0 * ka, 64, sign)
            hold_ref[0, ka * 8 + n0] = real
            hold_ref[1, ka * 8 + n0] = imag
    for ka in range(8):
        values = [(hold_ref[0, ka * 8 + n0], hold_ref[1, ka * 8 + n0]) for n0 in range(8)]
        for kb, value in enumerate(transform(values, sign)):
            store(ka + 8 * kb, value)


def middle_kernel(
    refs_ref,
    shift_ref,
    in_hbm,
    forward_hbm,
    inverse_hbm,
    twiddle_hbm,
    out_hbm,
    in_ref,
    out_ref,
    forward_ref,
    inverse_ref,
    twiddle_ref,
    mid_ref,
    back_ref,
    hold_ref,
    sems,
):
    waits = fetch(
        [twiddle_hbm] + [in_hbm.at[:, n] for n in range(8)] + [forward_hbm, inverse_hbm],
        [twiddle_ref] + [in_ref.at[:, n] for n in range(8)] + [forward_ref, inverse_ref],
        sems,
    )
    waits[0].wait()
    early = lax.broadcasted_iota(jnp.int32, (8, 128), 1) % 32 < 16
    for tile in range(2):
        sub = 8 * tile

        def load(s, sub=sub):
            if sub == 0 and s < 8:
                waits[1 + s].wait()
            return in_ref[s // 8, s % 8, sub : sub + 8, :], in_ref[s // 8, s % 8, 16 + sub : 24 + sub, :]

        def store(m1, value, sub=sub):
            real, imag = value
            tr, ti = twiddle_ref[0, m1 : m1 + 1, :], twiddle_ref[1, m1 : m1 + 1, :]
            at = m1 * 16 + sub
            mid_ref[at : at + 8, 0:128] = real * tr - imag * ti
            mid_ref[at : at + 8, 128:256] = real * ti + imag * tr

        column_transform(load, store, -1, hold_ref.at[0])
    waits[9].wait()
    waits[10].wait()
    forward, inverse = forward_ref[...], inverse_ref[...]
    for part in range(4):
        rows = slice(256 * part, 256 * part + 256)
        spectrum = matmul(spread(mid_ref[rows, :]), forward, ((1,), (0,)))
        real, imag = spectrum[:, :128], spectrum[:, 128:]
        for ref in range(2):
            cosine, sine = shift_ref[2 * ref, rows, :], shift_ref[2 * ref + 1, rows, :]
            turned = jnp.concatenate([real * cosine - imag * sine, real * sine + imag * cosine], axis=1)
            back_ref[ref, rows, :] = matmul(spread(turned), inverse, ((1,), (0,)))
    leaving = []
    for tile in range(2):
        sub = 8 * tile
        for ref in range(2):

            def load(m1, ref=ref, sub=sub):
                at = m1 * 16 + sub
                real, imag = back_ref[ref, at : at + 8, 0:128], back_ref[ref, at : at + 8, 128:256]
                tr, ti = twiddle_ref[0, m1 : m1 + 1, :], twiddle_ref[1, m1 : m1 + 1, :]
                return real * tr + imag * ti, imag * tr - real * ti

            if ref == 0:

                def store(s, value, sub=sub):
                    out_ref[s // 8, s % 8, sub : sub + 8, :] = value[0]
                    out_ref[s // 8, s % 8, 16 + sub : 24 + sub, :] = value[1]

            else:

                def store(s, value, sub=sub):
                    chosen = jnp.where(early, refs_ref[0, 2 * s], refs_ref[0, 2 * s + 1]) > 0
                    for c in range(2):
                        at = (s // 8, s % 8, slice(16 * c + sub, 16 * c + sub + 8))
                        out_ref[at] = jnp.where(chosen, value[c], out_ref[at])
                    if sub == 8 and s >= 56:
                        copy = pltpu.make_async_copy(
                            out_ref.at[:, s % 8], out_hbm.at[:, s % 8], sems.at[11 + s % 8]
                        )
                        copy.start()
                        leaving.append(copy)

            column_transform(load, store, 1, hold_ref.at[ref])
    for copy in leaving:
        copy.wait()


def inverse_y_kernel(place_ref, in_ref, phase_ref, coupling_ref, matrix_ref, twiddle_ref, out_ref, *rest):
    first_ref, last_ref, image_refs, mid_ref, image_hold = rest[0], rest[1], rest[2:6], rest[6], rest[7]
    matrix = matrix_ref[...]
    for p in range(8):
        block = in_ref[8 * p : 8 * p + 8].reshape(256, 128)
        mid_ref[128 * p : 128 * p + 128, :] = matmul(spread(block.T), matrix, ((1,), (0,)))
    for field in range(2):
        for tile in range(4):
            rows = slice(8 * tile, 8 * tile + 8)
            values = []
            for k1 in range(NY_A):
                at = k1 * 64 + field * 32 + tile * 8
                real, imag = mid_ref[at : at + 8, 0:128], mid_ref[at : at + 8, 128:256]
                if k1:
                    tr, ti = twiddle_ref[0, k1 : k1 + 1, :], twiddle_ref[1, k1 : k1 + 1, :]
                    real, imag = real * tr + imag * ti, imag * tr - real * ti
                values.append((real, imag))
            for a, (real, imag) in enumerate(transform(values, 1)):
                lanes = slice(128 * a, 128 * a + 128)
                cosine, sine = phase_ref[0, rows, lanes], phase_ref[1, rows, lanes]
                if field == 0:
                    real, imag = real * cosine + imag * sine, imag * cosine - real * sine
                else:
                    real, imag = real * cosine - imag * sine, imag * cosine + real * sine
                for c, value in enumerate((real, imag)):
                    out_ref[field, c, rows, lanes] = value
                    row = 2 * field + c
                    if tile == 0:
                        first_ref[row : row + 1, lanes] = value[0:1]
                    if tile == 3:
                        last_ref[row : row + 1, lanes] = value[7:8]
    row = lax.broadcasted_iota(jnp.int32, (8, 2048), 0)
    for tile, source, receiver in corrected(out_ref, None, None, coupling_ref):
        image = source[0] * receiver[0] + source[1] * receiver[1]
        if tile == 0:
            image = jnp.where(row == 0, 0.0, image)
        if tile == 3:
            image = jnp.where(row == 7, 0.0, image)
        image_hold[8 * tile : 8 * tile + 8, :] = image
    place = place_ref[0]
    for k in range(4):
        at = pl.multiple_of(((place + k) % 4) * 8, 8)
        image_refs[k][...] = image_hold[pl.ds(at, 8), :]


def laplace_kernel(wave_ref, above_ref, below_ref, coupling_ref, out_ref, edge_ref):
    for tile, source, receiver in corrected(wave_ref, above_ref, below_ref, coupling_ref):
        rows = slice(8 * tile, 8 * tile + 8)
        for field, pair in enumerate((source, receiver)):
            out_ref[field, 0, 0, rows, :] = pair[0]
            out_ref[field, 0, 1, rows, :] = pair[1]
        image = source[0] * receiver[0] + source[1] * receiver[1]
        for part in range(4):
            lanes = slice(512 * part, 512 * part + 512)
            if tile == 0:
                edge_ref[part : part + 1, :] = image[0:1, lanes]
            if tile == 3:
                edge_ref[4 + part : 5 + part, :] = image[7:8, lanes]


def corrected(wave_ref, above_ref, below_ref, coupling_ref):
    row = lax.broadcasted_iota(jnp.int32, (8, 2048), 0)
    lane = lax.broadcasted_iota(jnp.int32, (8, 2048), 1)
    for tile in range(4):
        rows = slice(8 * tile, 8 * tile + 8)
        coupling = coupling_ref[rows, :]
        results = []
        for field in range(2):
            laplace = []
            for c in range(2):
                value = wave_ref[field, c, rows, :]
                index = 2 * field + c
                if tile > 0:
                    before = wave_ref[field, c, 8 * tile - 1 : 8 * tile, :]
                else:
                    before = 0.0 if above_ref is None else above_ref[index : index + 1, :]
                if tile < 3:
                    after = wave_ref[field, c, 8 * tile + 8 : 8 * tile + 9, :]
                else:
                    after = 0.0 if below_ref is None else below_ref[index : index + 1, :]
                up = jnp.where(row == 0, before, pltpu.roll(value, 1, 0))
                down = jnp.where(row == 7, after, pltpu.roll(value, 7, 0))
                left = jnp.where(lane == 0, 0.0, pltpu.roll(value, 1, 1))
                right = jnp.where(lane == 2047, 0.0, pltpu.roll(value, 2047, 1))
                laplace.append(up + down + left + right - 4.0 * value)
            sign = -1.0 if field == 0 else 1.0
            scaled = coupling * sign
            real = wave_ref[field, 0, rows, :] - scaled * laplace[1]
            imag = wave_ref[field, 1, rows, :] + scaled * laplace[0]
            results.append((real, imag))
        yield tile, results[0], results[1]


def assemble_kernel(place_ref, own_ref, *rest):
    refs, out_ref = (own_ref,) + rest[:3], rest[3]
    place = place_ref[0]
    for k, ref in enumerate(refs):
        at = pl.multiple_of(((place + 4 - k) % 4) * 8, 8)
        out_ref[0, pl.ds(at, 8), :] = ref[:, 0:2048]
    if own_ref.shape[1] > 2048:
        edges = [ref[:, 2048:2560] for ref in refs]
        total = edges[0] + edges[1] + edges[2] + edges[3]
        for part in range(4):
            lanes = slice(512 * part, 512 * part + 512)
            out_ref[0, 0:1, lanes] = total[part : part + 1]
            out_ref[0, 31:32, lanes] = total[4 + part : 5 + part]


def whole(memory=pltpu.VMEM):
    return pl.BlockSpec(memory_space=memory)


def f32(*shape):
    return jax.ShapeDtypeStruct(shape, jnp.float32)


def call(kernel, out_shape, operands, scratch=(), smem=0, far=0, near=(), near_out=False, far_out=False):
    hbm = whole(pl.ANY if INTERPRET else pltpu.HBM)
    many = isinstance(out_shape, (tuple, list))
    if not INTERPRET:
        operands = tuple(
            pltpu.with_memory_space_constraint(x, pltpu.VMEM)
            if i in near
            else pltpu.with_memory_space_constraint(x, pltpu.HBM) if i >= len(operands) - far else x
            for i, x in enumerate(operands)
        )
        if near_out:
            shapes = out_shape if many else (out_shape,)
            shapes = tuple(pltpu.VMEM(x.shape, x.dtype) for x in shapes)
            out_shape = shapes if many else shapes[0]
        if far_out:
            out_shape = pltpu.HBM(out_shape.shape, out_shape.dtype)
    return pl.pallas_call(
        kernel,
        out_shape=out_shape,
        in_specs=[whole(pltpu.SMEM)] * smem
        + [whole()] * (len(operands) - smem - far)
        + [hbm] * far,
        out_specs=[whole()] * len(out_shape) if many else hbm if far_out else whole(),
        scratch_shapes=list(scratch),
        interpret=INTERPRET,
        compiler_params=pltpu.CompilerParams(vmem_limit_bytes=VMEM_BYTES),
    )(*operands)


def forward_y(wavefields):
    const = constants()
    return call(
        forward_y_kernel,
        f32(64, 32, 128),
        (wavefields, jnp.asarray(const["y_forward"]), jnp.asarray(const["y_twiddle"])),
        (
            pltpu.VMEM((2, 1, 2, 32, 2048), jnp.float32),
            pltpu.VMEM((256, 768), BF16),
            pltpu.VMEM((2, 16, 128), jnp.float32),
            pltpu.VMEM((1024, 256), jnp.float32),
            pltpu.SemaphoreType.DMA((10,)),
        ),
        far=3,
        near_out=True,
    )


def middle(blocks, shift, ref_index):
    const = constants()
    blocks = call(
        middle_kernel,
        f32(8, 8, 32, 128),
        (
            ref_index,
            shift,
            blocks.reshape(8, 8, 32, 128),
            jnp.asarray(const["x_forward"]),
            jnp.asarray(const["x_inverse"]),
            jnp.asarray(const["x_twiddle"]),
        ),
        (
            pltpu.VMEM((8, 8, 32, 128), jnp.float32),
            pltpu.VMEM((8, 8, 32, 128), jnp.float32),
            pltpu.VMEM((768, 256), BF16),
            pltpu.VMEM((768, 256), BF16),
            pltpu.VMEM((2, 64, 128), jnp.float32),
            pltpu.VMEM((1024, 256), jnp.float32),
            pltpu.VMEM((2, 1024, 256), jnp.float32),
            pltpu.VMEM((2, 2, 64, 8, 128), jnp.float32),
            pltpu.SemaphoreType.DMA((19,)),
        ),
        smem=1,
        far=4,
        near=(1,),
        far_out=True,
    )
    return blocks.reshape(64, 32, 128)


def inverse_y(place, blocks, phase, coupling):
    const = constants()
    return call(
        inverse_y_kernel,
        (f32(2, 2, 32, 2048),) + (f32(4, 2048),) * 2 + (f32(8, 2048),) * 4,
        (place, blocks, phase, coupling, jnp.asarray(const["y_inverse"]), jnp.asarray(const["y_twiddle"])),
        (pltpu.VMEM((1024, 256), jnp.float32), pltpu.VMEM((32, 2048), jnp.float32)),
        smem=1,
        near=(1, 2, 3),
        near_out=True,
    )


def laplace(wave, above, below, coupling):
    return call(
        laplace_kernel,
        (f32(2, 1, 2, 32, 2048), f32(8, 512)),
        (wave, above, below, coupling),
        near=(0, 1, 2, 3),
    )


def assemble(place, pieces):
    return call(assemble_kernel, f32(1, 32, 2048), (place,) + tuple(pieces), smem=1)


def wave_values(number, length):
    signed = jnp.where(number < length // 2, number, number - length)
    return 2.0 * math.pi / length * signed.astype(jnp.float32)


def shift_tables(space_index, omega, ref_velocity):
    row = lax.broadcasted_iota(jnp.int32, (1024, 128), 0)
    lane = lax.broadcasted_iota(jnp.int32, (1024, 128), 1)
    kx = wave_values(row // 16 + 64 * (lane % 32), NX)
    k1 = 2 * (space_index // 8) + lane // 64
    k2 = 16 * (space_index % 8) + row % 16
    ky = wave_values(k1 + 16 * k2, NY)
    sign = jnp.where((lane // 32) % 2 == 0, -1.0, 1.0).astype(jnp.float32)
    squared = kx**2 + ky**2
    tables = []
    for ref in range(2):
        vertical = (omega / ref_velocity[ref]) ** 2 - squared
        root = DZ * jnp.sqrt(jnp.abs(vertical))
        travels = vertical >= 0.0
        tables.append(jnp.where(travels, jnp.cos(root), jnp.exp(-root)))
        tables.append(jnp.where(travels, sign * jnp.sin(root), 0.0))
    return jnp.stack(tables)


def phase_tables(speed, ref_rows, omega):
    time_shift = omega * DZ * (1.0 / speed - 1.0 / ref_rows)
    return jnp.stack([jnp.cos(time_shift), jnp.sin(time_shift)])


def coupling_table(speed, ref_rows, omega):
    return DZ * (speed - ref_rows) * ref_rows / (16.0 * omega)


def shifted_pairs(step, count=4):
    return [(i, (i + step) % count) for i in range(count)]


def slab_speed(velocity, owner, freq_index):
    stored = lax.dynamic_index_in_dim(velocity, owner % 4, 0, keepdims=False).reshape(4, 8, 2048)
    source = owner // 4
    mine = lax.dynamic_index_in_dim(stored, freq_index, 0, keepdims=False)
    for step in (1, 2, 3):
        piece = lax.dynamic_index_in_dim(stored, (freq_index + step) % 4, 0, keepdims=False)
        arrived = lax.ppermute(piece, "freq", shifted_pairs(step))
        mine = jnp.where((freq_index + 4 - step) % 4 == source, arrived, mine)
    return gathered(mine)


def gathered(mine):
    pieces = [mine]
    for step in (1, 2, 3):
        pieces.append(lax.ppermute(mine, "freq", shifted_pairs(step)))
    return pieces


def exchange(blocks):
    return lax.all_to_all(blocks, "space", split_axis=0, concat_axis=0, tiled=True)


def step_down(wavefields, frequencies, velocity, slab_owner, ref_velocity, ref_index):
    space_index = lax.axis_index("space")
    freq_index = lax.axis_index("freq")
    place = freq_index.reshape(1).astype(jnp.int32)
    omega = frequencies[0]
    slab = slab_speed(velocity, slab_owner[0], freq_index)
    blocks = forward_y(wavefields)
    blocks = exchange(blocks)
    shift = shift_tables(space_index, omega, ref_velocity[0])
    speed = assemble(place, slab)[0]
    local_refs = lax.dynamic_slice_in_dim(ref_index[0], 2 * space_index, 2)
    ref_rows = jnp.repeat(ref_velocity[0][local_refs], 16)[:, None]
    phase = phase_tables(speed, ref_rows, omega)
    coupling = coupling_table(speed, ref_rows, omega)
    blocks = middle(blocks, shift, ref_index)
    blocks = exchange(blocks)
    wave, first, last, *quarters = inverse_y(place, blocks, phase, coupling)
    count = 64
    above = lax.ppermute(last, "space", [(i, i + 1) for i in range(count - 1)])
    below = lax.ppermute(first, "space", [(i + 1, i) for i in range(count - 1)])
    total = quarters[0]
    for step in (1, 2, 3):
        arrived = lax.ppermute(quarters[step], "freq", shifted_pairs(step))
        total = total + arrived
    fields, edges = laplace(wave, above, below, coupling)
    image = assemble(place, gathered(jnp.concatenate([total, edges], axis=1)))
    return fields, image


def solution(mesh):
    in_specs = (
        P(None, "freq", None, "space", None),
        P("freq"),
        P("freq", "space", None),
        P(),
        P(),
        P(),
    )
    out_specs = (P(None, "freq", None, "space", None), P(None, "space", None))
    return jax.shard_map(step_down, mesh=mesh, in_specs=in_specs, out_specs=out_specs, check_vma=False)
```

```python
import functools
import math

import jax
import jax.numpy as jnp
import numpy as np
from jax import lax
from jax.experimental import pallas as pl
from jax.experimental.pallas import tpu as pltpu
from jax.sharding import PartitionSpec as P


DZ = 4
INTERPRET = False
VMEM_BYTES = 20 * 2**20
BF16 = jnp.bfloat16

NY_A, NY_B = 16, 128
NX_S, NX_R = 64, 32
NY, NX = NY_A * NY_B, NX_S * NX_R


def split_bf16(matrix):
    high = np.asarray(matrix, np.float32).astype(BF16)
    low = (np.asarray(matrix, np.float64) - high.astype(np.float64)).astype(np.float32).astype(BF16)
    return high, low


@functools.cache
def constants():
    k2 = np.arange(NY_B)
    b = np.arange(NY_B)
    angle = 2.0 * np.pi * (np.outer(k2, b) % NY_B) / NY_B
    cosine, sine = np.cos(angle), np.sin(angle)
    forward = np.stack(
        [np.concatenate([cosine, sine], 1), np.concatenate([-sine, cosine], 1)], 0
    )
    forward = forward.reshape(2, 8, 16, 256).transpose(1, 0, 2, 3).reshape(256, 256)
    inverse = forward.copy() / NY
    fh, fl = split_bf16(forward)
    y_forward = np.concatenate([fh, fl, fh], 1)
    ih, il = split_bf16(inverse)
    y_inverse = np.concatenate([ih, il, ih], 0)
    r = np.arange(NX_R)
    angle = 2.0 * np.pi * (np.outer(r, r) % NX_R) / NX_R
    cosine = np.kron(np.eye(4), np.cos(angle))
    sine = np.kron(np.eye(4), np.sin(angle))
    x_forward = np.block([[cosine, -sine], [sine, cosine]])
    x_inverse = np.block([[cosine, sine], [-sine, cosine]]) / NX
    xh, xl = split_bf16(x_forward)
    x_forward = np.concatenate([xh, xl, xh], 0)
    xh, xl = split_bf16(x_inverse)
    x_inverse = np.concatenate([xh, xl, xh], 0)
    angle = 2.0 * np.pi * np.outer(np.arange(NY_A), b) / NY
    y_twiddle = np.stack([np.cos(angle), -np.sin(angle)]).astype(np.float32)
    angle = 2.0 * np.pi * np.outer(np.arange(NX_S), np.tile(r, 4)) / NX
    x_twiddle = np.stack([np.cos(angle), -np.sin(angle)]).astype(np.float32)
    return dict(
        y_forward=y_forward,
        y_inverse=y_inverse,
        x_forward=x_forward,
        x_inverse=x_inverse,
        y_twiddle=y_twiddle,
        x_twiddle=x_twiddle,
    )


def times(value, numerator, length, sign):
    real, imag = value
    turn = (sign * numerator) % length
    eighth = turn * 8
    if turn == 0:
        return real, imag
    if eighth % length == 0:
        step = eighth // length
        half = math.sqrt(0.5)
        if step == 2:
            return -imag, real
        if step == 4:
            return -real, -imag
        if step == 6:
            return imag, -real
        if step == 1:
            return (real - imag) * half, (real + imag) * half
        if step == 3:
            return (real + imag) * -half, (real - imag) * half
        if step == 5:
            return (imag - real) * half, (real + imag) * -half
        return (real + imag) * half, (imag - real) * half
    cosine = math.cos(2.0 * math.pi * turn / length)
    sine = math.sin(2.0 * math.pi * turn / length)
    return real * cosine - imag * sine, real * sine + imag * cosine


def plus(left, right):
    return left[0] + right[0], left[1] + right[1]


def minus(left, right):
    return left[0] - right[0], left[1] - right[1]


def transform(values, sign):
    length = len(values)
    if length == 1:
        return values
    if length == 2:
        return [plus(values[0], values[1]), minus(values[0], values[1])]
    if length == 4:
        even_sum, even_diff = plus(values[0], values[2]), minus(values[0], values[2])
        odd_sum, odd_diff = plus(values[1], values[3]), minus(values[1], values[3])
        if sign > 0:
            first = (even_diff[0] - odd_diff[1], even_diff[1] + odd_diff[0])
            third = (even_diff[0] + odd_diff[1], even_diff[1] - odd_diff[0])
        else:
            first = (even_diff[0] + odd_diff[1], even_diff[1] - odd_diff[0])
            third = (even_diff[0] - odd_diff[1], even_diff[1] + odd_diff[0])
        return [plus(even_sum, odd_sum), first, minus(even_sum, odd_sum), third]
    radix = 4 if length % 4 == 0 and length > 8 else 2
    rest = length // radix
    columns = [transform(values[i::radix], sign) for i in range(radix)]
    result = [None] * length
    for k in range(rest):
        picked = [times(columns[i][k], i * k, length, sign) for i in range(radix)]
        for q, value in enumerate(transform(picked, sign)):
            result[k + rest * q] = value
    return result


def spread(value):
    high = value.astype(BF16)
    low = (value - high.astype(jnp.float32)).astype(BF16)
    return jnp.concatenate([high, high, low], axis=1)


def matmul(left, right, contract):
    return lax.dot_general(left, right, (contract, ((), ())), preferred_element_type=jnp.float32)


def fetch(sources, targets, sems):
    copies = [pltpu.make_async_copy(s, t, sems.at[i]) for i, (s, t) in enumerate(zip(sources, targets))]
    for copy in copies:
        copy.start()
    return copies


def forward_y_kernel(wave_hbm, matrix_hbm, twiddle_hbm, out_ref, wave_ref, matrix_ref, twiddle_ref, mid_ref, sems):
    parts = [(field, slice(8 * tile, 8 * tile + 8)) for field in range(2) for tile in range(4)]
    views = [[ref.at[field, 0, :, rows, :] for field, rows in parts] for ref in (wave_hbm, wave_ref)]
    waits = fetch([twiddle_hbm] + views[0] + [matrix_hbm], [twiddle_ref] + views[1] + [matrix_ref], sems)
    waits[0].wait()
    for field in range(2):
        for tile in range(4):
            waits[1 + 4 * field + tile].wait()
            rows = slice(8 * tile, 8 * tile + 8)
            values = [
                tuple(wave_ref[field, 0, c, rows, 128 * a : 128 * a + 128] for c in range(2))
                for a in range(NY_A)
            ]
            for k1, (real, imag) in enumerate(transform(values, -1)):
                if k1:
                    tr, ti = twiddle_ref[0, k1 : k1 + 1, :], twiddle_ref[1, k1 : k1 + 1, :]
                    real, imag = real * tr - imag * ti, real * ti + imag * tr
                at = k1 * 64 + field * 32 + tile * 8
                mid_ref[at : at + 8, 0:128] = real
                mid_ref[at : at + 8, 128:256] = imag
    waits[9].wait()
    matrix = matrix_ref[...]
    for pair in range(4):
        packed = spread(mid_ref[256 * pair : 256 * pair + 256, :])
        product = matmul(matrix, packed, ((1,), (1,)))
        for half in range(2):
            at = 16 * pair + 8 * half
            out_ref[at : at + 8] = product[:, 128 * half : 128 * half + 128].reshape(8, 32, 128)


def column_transform(load, store, sign, hold_ref):
    for n0 in range(8):
        piece = transform([load(8 * n1 + n0) for n1 in range(8)], sign)
        for ka in range(8):
            real, imag = times(piece[ka], n0 * ka, 64, sign)
            hold_ref[0, ka * 8 + n0] = real
            hold_ref[1, ka * 8 + n0] = imag
    for ka in range(8):
        values = [(hold_ref[0, ka * 8 + n0], hold_ref[1, ka * 8 + n0]) for n0 in range(8)]
        for kb, value in enumerate(transform(values, sign)):
            store(ka + 8 * kb, value)


def middle_kernel(
    refs_ref,
    shift_ref,
    in_hbm,
    forward_hbm,
    inverse_hbm,
    twiddle_hbm,
    out_hbm,
    in_ref,
    out_ref,
    forward_ref,
    inverse_ref,
    twiddle_ref,
    mid_ref,
    back_ref,
    hold_ref,
    sems,
):
    waits = fetch(
        [twiddle_hbm] + [in_hbm.at[:, n] for n in range(8)] + [forward_hbm, inverse_hbm],
        [twiddle_ref] + [in_ref.at[:, n] for n in range(8)] + [forward_ref, inverse_ref],
        sems,
    )
    waits[0].wait()
    early = lax.broadcasted_iota(jnp.int32, (8, 128), 1) % 32 < 16
    for tile in range(2):
        sub = 8 * tile

        def load(s, sub=sub):
            if sub == 0 and s < 8:
                waits[1 + s].wait()
            return in_ref[s // 8, s % 8, sub : sub + 8, :], in_ref[s // 8, s % 8, 16 + sub : 24 + sub, :]

        def store(m1, value, sub=sub):
            real, imag = value
            tr, ti = twiddle_ref[0, m1 : m1 + 1, :], twiddle_ref[1, m1 : m1 + 1, :]
            at = m1 * 16 + sub
            mid_ref[at : at + 8, 0:128] = real * tr - imag * ti
            mid_ref[at : at + 8, 128:256] = real * ti + imag * tr

        column_transform(load, store, -1, hold_ref.at[0])
    waits[9].wait()
    waits[10].wait()
    forward, inverse = forward_ref[...], inverse_ref[...]
    for part in range(4):
        rows = slice(256 * part, 256 * part + 256)
        spectrum = matmul(spread(mid_ref[rows, :]), forward, ((1,), (0,)))
        real, imag = spectrum[:, :128], spectrum[:, 128:]
        for ref in range(2):
            cosine, sine = shift_ref[2 * ref, rows, :], shift_ref[2 * ref + 1, rows, :]
            turned = jnp.concatenate([real * cosine - imag * sine, real * sine + imag * cosine], axis=1)
            back_ref[ref, rows, :] = matmul(spread(turned), inverse, ((1,), (0,)))
    leaving = []
    for tile in range(2):
        sub = 8 * tile
        for ref in range(2):

            def load(m1, ref=ref, sub=sub):
                at = m1 * 16 + sub
                real, imag = back_ref[ref, at : at + 8, 0:128], back_ref[ref, at : at + 8, 128:256]
                tr, ti = twiddle_ref[0, m1 : m1 + 1, :], twiddle_ref[1, m1 : m1 + 1, :]
                return real * tr + imag * ti, imag * tr - real * ti

            if ref == 0:

                def store(s, value, sub=sub):
                    out_ref[s // 8, s % 8, sub : sub + 8, :] = value[0]
                    out_ref[s // 8, s % 8, 16 + sub : 24 + sub, :] = value[1]

            else:

                def store(s, value, sub=sub):
                    chosen = jnp.where(early, refs_ref[0, 2 * s], refs_ref[0, 2 * s + 1]) > 0
                    for c in range(2):
                        at = (s // 8, s % 8, slice(16 * c + sub, 16 * c + sub + 8))
                        out_ref[at] = jnp.where(chosen, value[c], out_ref[at])
                    if sub == 8 and s >= 56:
                        copy = pltpu.make_async_copy(
                            out_ref.at[:, s % 8], out_hbm.at[:, s % 8], sems.at[11 + s % 8]
                        )
                        copy.start()
                        leaving.append(copy)

            column_transform(load, store, 1, hold_ref.at[ref])
    for copy in leaving:
        copy.wait()


def inverse_y_kernel(place_ref, in_ref, phase_ref, coupling_ref, matrix_ref, twiddle_ref, out_ref, *rest):
    first_ref, last_ref, image_refs, mid_ref, image_hold = rest[0], rest[1], rest[2:6], rest[6], rest[7]
    matrix = matrix_ref[...]
    for p in range(8):
        block = in_ref[8 * p : 8 * p + 8].reshape(256, 128)
        mid_ref[128 * p : 128 * p + 128, :] = matmul(spread(block.T), matrix, ((1,), (0,)))
    for field in range(2):
        for tile in range(4):
            rows = slice(8 * tile, 8 * tile + 8)
            values = []
            for k1 in range(NY_A):
                at = k1 * 64 + field * 32 + tile * 8
                real, imag = mid_ref[at : at + 8, 0:128], mid_ref[at : at + 8, 128:256]
                if k1:
                    tr, ti = twiddle_ref[0, k1 : k1 + 1, :], twiddle_ref[1, k1 : k1 + 1, :]
                    real, imag = real * tr + imag * ti, imag * tr - real * ti
                values.append((real, imag))
            for a, (real, imag) in enumerate(transform(values, 1)):
                lanes = slice(128 * a, 128 * a + 128)
                cosine, sine = phase_ref[0, rows, lanes], phase_ref[1, rows, lanes]
                if field == 0:
                    real, imag = real * cosine + imag * sine, imag * cosine - real * sine
                else:
                    real, imag = real * cosine - imag * sine, imag * cosine + real * sine
                for c, value in enumerate((real, imag)):
                    out_ref[field, c, rows, lanes] = value
                    row = 2 * field + c
                    if tile == 0:
                        first_ref[row : row + 1, lanes] = value[0:1]
                    if tile == 3:
                        last_ref[row : row + 1, lanes] = value[7:8]
    row = lax.broadcasted_iota(jnp.int32, (8, 2048), 0)
    for tile, source, receiver in corrected(out_ref, None, None, coupling_ref):
        image = source[0] * receiver[0] + source[1] * receiver[1]
        if tile == 0:
            image = jnp.where(row == 0, 0.0, image)
        if tile == 3:
            image = jnp.where(row == 7, 0.0, image)
        image_hold[8 * tile : 8 * tile + 8, :] = image
    place = place_ref[0]
    for k in range(4):
        at = pl.multiple_of(((place + k) % 4) * 8, 8)
        image_refs[k][...] = image_hold[pl.ds(at, 8), :]


def laplace_kernel(index_ref, wave_ref, above_ref, below_ref, coupling_ref, out_ref, edge_ref):
    index = jnp.full((1, 2048), index_ref[0], jnp.int32)
    above = [jnp.where(index == 0, 0.0, above_ref[row : row + 1, :]) for row in range(4)]
    below = [jnp.where(index == 63, 0.0, below_ref[row : row + 1, :]) for row in range(4)]
    for tile, source, receiver in corrected(wave_ref, above, below, coupling_ref):
        rows = slice(8 * tile, 8 * tile + 8)
        for field, pair in enumerate((source, receiver)):
            out_ref[field, 0, 0, rows, :] = pair[0]
            out_ref[field, 0, 1, rows, :] = pair[1]
        image = source[0] * receiver[0] + source[1] * receiver[1]
        for part in range(4):
            lanes = slice(512 * part, 512 * part + 512)
            if tile == 0:
                edge_ref[part : part + 1, :] = image[0:1, lanes]
            if tile == 3:
                edge_ref[4 + part : 5 + part, :] = image[7:8, lanes]


def corrected(wave_ref, above, below, coupling_ref):
    row = lax.broadcasted_iota(jnp.int32, (8, 2048), 0)
    lane = lax.broadcasted_iota(jnp.int32, (8, 2048), 1)
    for tile in range(4):
        rows = slice(8 * tile, 8 * tile + 8)
        coupling = coupling_ref[rows, :]
        results = []
        for field in range(2):
            laplace = []
            for c in range(2):
                value = wave_ref[field, c, rows, :]
                index = 2 * field + c
                if tile > 0:
                    before = wave_ref[field, c, 8 * tile - 1 : 8 * tile, :]
                else:
                    before = 0.0 if above is None else above[index]
                if tile < 3:
                    after = wave_ref[field, c, 8 * tile + 8 : 8 * tile + 9, :]
                else:
                    after = 0.0 if below is None else below[index]
                up = jnp.where(row == 0, before, pltpu.roll(value, 1, 0))
                down = jnp.where(row == 7, after, pltpu.roll(value, 7, 0))
                left = jnp.where(lane == 0, 0.0, pltpu.roll(value, 1, 1))
                right = jnp.where(lane == 2047, 0.0, pltpu.roll(value, 2047, 1))
                laplace.append(up + down + left + right - 4.0 * value)
            sign = -1.0 if field == 0 else 1.0
            scaled = coupling * sign
            real = wave_ref[field, 0, rows, :] - scaled * laplace[1]
            imag = wave_ref[field, 1, rows, :] + scaled * laplace[0]
            results.append((real, imag))
        yield tile, results[0], results[1]


def assemble_kernel(place_ref, own_ref, *rest):
    refs, out_ref = (own_ref,) + rest[:3], rest[3]
    place = place_ref[0]
    for k, ref in enumerate(refs):
        at = pl.multiple_of(((place + 4 - k) % 4) * 8, 8)
        out_ref[0, pl.ds(at, 8), :] = ref[:, 0:2048]
    if own_ref.shape[1] > 2048:
        edges = [ref[:, 2048:2560] for ref in refs]
        total = edges[0] + edges[1] + edges[2] + edges[3]
        for part in range(4):
            lanes = slice(512 * part, 512 * part + 512)
            out_ref[0, 0:1, lanes] = total[part : part + 1]
            out_ref[0, 31:32, lanes] = total[4 + part : 5 + part]


def whole(memory=pltpu.VMEM):
    return pl.BlockSpec(memory_space=memory)


def f32(*shape):
    return jax.ShapeDtypeStruct(shape, jnp.float32)


def call(kernel, out_shape, operands, scratch=(), smem=0, far=0, near=(), near_out=False, far_out=False):
    hbm = whole(pl.ANY if INTERPRET else pltpu.HBM)
    many = isinstance(out_shape, (tuple, list))
    if not INTERPRET:
        operands = tuple(
            pltpu.with_memory_space_constraint(x, pltpu.VMEM)
            if i in near
            else pltpu.with_memory_space_constraint(x, pltpu.HBM) if i >= len(operands) - far else x
            for i, x in enumerate(operands)
        )
        if near_out:
            shapes = out_shape if many else (out_shape,)
            shapes = tuple(pltpu.VMEM(x.shape, x.dtype) for x in shapes)
            out_shape = shapes if many else shapes[0]
        if far_out:
            out_shape = pltpu.HBM(out_shape.shape, out_shape.dtype)
    return pl.pallas_call(
        kernel,
        out_shape=out_shape,
        in_specs=[whole(pltpu.SMEM)] * smem
        + [whole()] * (len(operands) - smem - far)
        + [hbm] * far,
        out_specs=[whole()] * len(out_shape) if many else hbm if far_out else whole(),
        scratch_shapes=list(scratch),
        interpret=INTERPRET,
        compiler_params=pltpu.CompilerParams(vmem_limit_bytes=VMEM_BYTES),
    )(*operands)


def forward_y(wavefields):
    const = constants()
    return call(
        forward_y_kernel,
        f32(64, 32, 128),
        (wavefields, jnp.asarray(const["y_forward"]), jnp.asarray(const["y_twiddle"])),
        (
            pltpu.VMEM((2, 1, 2, 32, 2048), jnp.float32),
            pltpu.VMEM((256, 768), BF16),
            pltpu.VMEM((2, 16, 128), jnp.float32),
            pltpu.VMEM((1024, 256), jnp.float32),
            pltpu.SemaphoreType.DMA((10,)),
        ),
        far=3,
        near_out=True,
    )


def middle(blocks, shift, ref_index):
    const = constants()
    blocks = call(
        middle_kernel,
        f32(8, 8, 32, 128),
        (
            ref_index,
            shift,
            blocks.reshape(8, 8, 32, 128),
            jnp.asarray(const["x_forward"]),
            jnp.asarray(const["x_inverse"]),
            jnp.asarray(const["x_twiddle"]),
        ),
        (
            pltpu.VMEM((8, 8, 32, 128), jnp.float32),
            pltpu.VMEM((8, 8, 32, 128), jnp.float32),
            pltpu.VMEM((768, 256), BF16),
            pltpu.VMEM((768, 256), BF16),
            pltpu.VMEM((2, 64, 128), jnp.float32),
            pltpu.VMEM((1024, 256), jnp.float32),
            pltpu.VMEM((2, 1024, 256), jnp.float32),
            pltpu.VMEM((2, 2, 64, 8, 128), jnp.float32),
            pltpu.SemaphoreType.DMA((19,)),
        ),
        smem=1,
        far=4,
        near=(1,),
        far_out=True,
    )
    return blocks.reshape(64, 32, 128)


def inverse_y(place, blocks, phase, coupling):
    const = constants()
    return call(
        inverse_y_kernel,
        (f32(2, 2, 32, 2048),) + (f32(4, 2048),) * 2 + (f32(8, 2048),) * 4,
        (place, blocks, phase, coupling, jnp.asarray(const["y_inverse"]), jnp.asarray(const["y_twiddle"])),
        (pltpu.VMEM((1024, 256), jnp.float32), pltpu.VMEM((32, 2048), jnp.float32)),
        smem=1,
        near=(1, 2, 3),
        near_out=True,
    )


def laplace(index, wave, above, below, coupling):
    return call(
        laplace_kernel,
        (f32(2, 1, 2, 32, 2048), f32(8, 512)),
        (index, wave, above, below, coupling),
        smem=1,
        near=(1, 2, 3, 4),
    )


def assemble(place, pieces):
    return call(assemble_kernel, f32(1, 32, 2048), (place,) + tuple(pieces), smem=1)


def wave_values(number, length):
    signed = jnp.where(number < length // 2, number, number - length)
    return 2.0 * math.pi / length * signed.astype(jnp.float32)


def shift_tables(space_index, omega, ref_velocity):
    row = lax.broadcasted_iota(jnp.int32, (1024, 128), 0)
    lane = lax.broadcasted_iota(jnp.int32, (1024, 128), 1)
    kx = wave_values(row // 16 + 64 * (lane % 32), NX)
    k1 = 2 * (space_index // 8) + lane // 64
    k2 = 16 * (space_index % 8) + row % 16
    ky = wave_values(k1 + 16 * k2, NY)
    sign = jnp.where((lane // 32) % 2 == 0, -1.0, 1.0).astype(jnp.float32)
    squared = kx**2 + ky**2
    tables = []
    for ref in range(2):
        vertical = (omega / ref_velocity[ref]) ** 2 - squared
        root = DZ * jnp.sqrt(jnp.abs(vertical))
        travels = vertical >= 0.0
        tables.append(jnp.where(travels, jnp.cos(root), jnp.exp(-root)))
        tables.append(jnp.where(travels, sign * jnp.sin(root), 0.0))
    return jnp.stack(tables)


def phase_tables(speed, ref_rows, omega):
    time_shift = omega * DZ * (1.0 / speed - 1.0 / ref_rows)
    return jnp.stack([jnp.cos(time_shift), jnp.sin(time_shift)])


def coupling_table(speed, ref_rows, omega):
    return DZ * (speed - ref_rows) * ref_rows / (16.0 * omega)


def shifted_pairs(step, count=4):
    return [(i, (i + step) % count) for i in range(count)]


def slab_speed(velocity, owner, freq_index):
    stored = lax.dynamic_index_in_dim(velocity, owner % 4, 0, keepdims=False).reshape(4, 8, 2048)
    source = owner // 4
    mine = lax.dynamic_index_in_dim(stored, freq_index, 0, keepdims=False)
    for step in (1, 2, 3):
        piece = lax.dynamic_index_in_dim(stored, (freq_index + step) % 4, 0, keepdims=False)
        arrived = lax.ppermute(piece, "freq", shifted_pairs(step))
        mine = jnp.where((freq_index + 4 - step) % 4 == source, arrived, mine)
    return gathered(mine)


def gathered(mine):
    pieces = [mine]
    for step in (1, 2, 3):
        pieces.append(lax.ppermute(mine, "freq", shifted_pairs(step)))
    return pieces


def exchange(blocks):
    return lax.all_to_all(blocks, "space", split_axis=0, concat_axis=0, tiled=True)


def step_down(wavefields, frequencies, velocity, slab_owner, ref_velocity, ref_index):
    space_index = lax.axis_index("space")
    freq_index = lax.axis_index("freq")
    place = freq_index.reshape(1).astype(jnp.int32)
    omega = frequencies[0]
    slab = slab_speed(velocity, slab_owner[0], freq_index)
    blocks = forward_y(wavefields)
    blocks = exchange(blocks)
    shift = shift_tables(space_index, omega, ref_velocity[0])
    speed = assemble(place, slab)[0]
    local_refs = lax.dynamic_slice_in_dim(ref_index[0], 2 * space_index, 2)
    ref_rows = jnp.repeat(ref_velocity[0][local_refs], 16)[:, None]
    phase = phase_tables(speed, ref_rows, omega)
    coupling = coupling_table(speed, ref_rows, omega)
    blocks = middle(blocks, shift, ref_index)
    blocks = exchange(blocks)
    wave, first, last, *quarters = inverse_y(place, blocks, phase, coupling)
    above = lax.ppermute(last, "space", shifted_pairs(1, 64))
    below = lax.ppermute(first, "space", shifted_pairs(63, 64))
    total = quarters[0]
    for step in (1, 2, 3):
        arrived = lax.ppermute(quarters[step], "freq", shifted_pairs(step))
        total = total + arrived
    index = space_index.reshape(1).astype(jnp.int32)
    fields, edges = laplace(index, wave, above, below, coupling)
    image = assemble(place, gathered(jnp.concatenate([total, edges], axis=1)))
    return fields, image


def solution(mesh):
    in_specs = (
        P(None, "freq", None, "space", None),
        P("freq"),
        P("freq", "space", None),
        P(),
        P(),
        P(),
    )
    out_specs = (P(None, "freq", None, "space", None), P(None, "space", None))
    return jax.shard_map(step_down, mesh=mesh, in_specs=in_specs, out_specs=out_specs, check_vma=False)
```

```python
import functools
import math

import jax
import jax.numpy as jnp
import numpy as np
from jax import lax
from jax.experimental import pallas as pl
from jax.experimental.pallas import tpu as pltpu
from jax.sharding import PartitionSpec as P


DZ = 4
INTERPRET = False
VMEM_BYTES = 20 * 2**20
BF16 = jnp.bfloat16

NY_A, NY_B = 16, 128
NX_S, NX_R = 64, 32
NY, NX = NY_A * NY_B, NX_S * NX_R


def split_bf16(matrix):
    high = np.asarray(matrix, np.float32).astype(BF16)
    low = (np.asarray(matrix, np.float64) - high.astype(np.float64)).astype(np.float32).astype(BF16)
    return high, low


@functools.cache
def constants():
    k2 = np.arange(NY_B)
    b = np.arange(NY_B)
    angle = 2.0 * np.pi * (np.outer(k2, b) % NY_B) / NY_B
    cosine, sine = np.cos(angle), np.sin(angle)
    forward = np.stack(
        [np.concatenate([cosine, sine], 1), np.concatenate([-sine, cosine], 1)], 0
    )
    forward = forward.reshape(2, 8, 16, 256).transpose(1, 0, 2, 3).reshape(256, 256)
    y_matrix = np.stack(split_bf16(forward))
    r = np.arange(NX_R)
    angle = 2.0 * np.pi * (np.outer(r, r) % NX_R) / NX_R
    cosine = np.kron(np.eye(4), np.cos(angle))
    sine = np.kron(np.eye(4), np.sin(angle))
    x_forward = np.block([[cosine, -sine], [sine, cosine]])
    x_matrix = np.stack(split_bf16(x_forward))
    angle = 2.0 * np.pi * np.outer(np.arange(NY_A), b) / NY
    y_twiddle = np.stack([np.cos(angle), -np.sin(angle)]).astype(np.float32)
    angle = 2.0 * np.pi * np.outer(np.arange(NX_S), np.tile(r, 4)) / NX
    x_twiddle = np.stack([np.cos(angle), -np.sin(angle)]).astype(np.float32)
    return dict(
        y_matrix=y_matrix,
        x_matrix=x_matrix,
        y_twiddle=y_twiddle,
        x_twiddle=x_twiddle,
    )


def times(value, numerator, length, sign):
    real, imag = value
    turn = (sign * numerator) % length
    eighth = turn * 8
    if turn == 0:
        return real, imag
    if eighth % length == 0:
        step = eighth // length
        half = math.sqrt(0.5)
        if step == 2:
            return -imag, real
        if step == 4:
            return -real, -imag
        if step == 6:
            return imag, -real
        if step == 1:
            return (real - imag) * half, (real + imag) * half
        if step == 3:
            return (real + imag) * -half, (real - imag) * half
        if step == 5:
            return (imag - real) * half, (real + imag) * -half
        return (real + imag) * half, (imag - real) * half
    cosine = math.cos(2.0 * math.pi * turn / length)
    sine = math.sin(2.0 * math.pi * turn / length)
    return real * cosine - imag * sine, real * sine + imag * cosine


def plus(left, right):
    return left[0] + right[0], left[1] + right[1]


def minus(left, right):
    return left[0] - right[0], left[1] - right[1]


def transform(values, sign):
    length = len(values)
    if length == 1:
        return values
    if length == 2:
        return [plus(values[0], values[1]), minus(values[0], values[1])]
    if length == 4:
        even_sum, even_diff = plus(values[0], values[2]), minus(values[0], values[2])
        odd_sum, odd_diff = plus(values[1], values[3]), minus(values[1], values[3])
        if sign > 0:
            first = (even_diff[0] - odd_diff[1], even_diff[1] + odd_diff[0])
            third = (even_diff[0] + odd_diff[1], even_diff[1] - odd_diff[0])
        else:
            first = (even_diff[0] + odd_diff[1], even_diff[1] - odd_diff[0])
            third = (even_diff[0] - odd_diff[1], even_diff[1] + odd_diff[0])
        return [plus(even_sum, odd_sum), first, minus(even_sum, odd_sum), third]
    radix = 4 if length % 4 == 0 and length > 8 else 2
    rest = length // radix
    columns = [transform(values[i::radix], sign) for i in range(radix)]
    result = [None] * length
    for k in range(rest):
        picked = [times(columns[i][k], i * k, length, sign) for i in range(radix)]
        for q, value in enumerate(transform(picked, sign)):
            result[k + rest * q] = value
    return result


def spread(value):
    high = value.astype(BF16)
    low = (value - high.astype(jnp.float32)).astype(BF16)
    return jnp.concatenate([high, high, low], axis=1)


def tripled(matrix_ref, axis):
    return jnp.concatenate([matrix_ref[0], matrix_ref[1], matrix_ref[0]], axis=axis)


def matmul(left, right, contract):
    return lax.dot_general(left, right, (contract, ((), ())), preferred_element_type=jnp.float32)


def fetch(sources, targets, sems):
    copies = [pltpu.make_async_copy(s, t, sems.at[i]) for i, (s, t) in enumerate(zip(sources, targets))]
    for copy in copies:
        copy.start()
    return copies


def forward_y_kernel(wave_hbm, matrix_hbm, twiddle_hbm, out_ref, wave_ref, matrix_ref, twiddle_ref, mid_ref, sems):
    parts = [(field, slice(8 * tile, 8 * tile + 8)) for field in range(2) for tile in range(4)]
    views = [[ref.at[field, 0, :, rows, :] for field, rows in parts] for ref in (wave_hbm, wave_ref)]
    waits = fetch([twiddle_hbm] + views[0] + [matrix_hbm], [twiddle_ref] + views[1] + [matrix_ref], sems)
    waits[0].wait()
    for field in range(2):
        for tile in range(4):
            waits[1 + 4 * field + tile].wait()
            rows = slice(8 * tile, 8 * tile + 8)
            values = [
                tuple(wave_ref[field, 0, c, rows, 128 * a : 128 * a + 128] for c in range(2))
                for a in range(NY_A)
            ]
            for k1, (real, imag) in enumerate(transform(values, -1)):
                if k1:
                    tr, ti = twiddle_ref[0, k1 : k1 + 1, :], twiddle_ref[1, k1 : k1 + 1, :]
                    real, imag = real * tr - imag * ti, real * ti + imag * tr
                at = k1 * 64 + field * 32 + tile * 8
                mid_ref[at : at + 8, 0:128] = real
                mid_ref[at : at + 8, 128:256] = imag
    waits[9].wait()
    matrix = tripled(matrix_ref, 1)
    for pair in range(4):
        packed = spread(mid_ref[256 * pair : 256 * pair + 256, :])
        product = matmul(matrix, packed, ((1,), (1,)))
        for half in range(2):
            at = 16 * pair + 8 * half
            out_ref[at : at + 8] = product[:, 128 * half : 128 * half + 128].reshape(8, 32, 128)


def middle_kernel(
    refs_ref,
    shift_ref,
    in_hbm,
    matrix_hbm,
    twiddle_hbm,
    out_hbm,
    in_ref,
    out_ref,
    matrix_ref,
    twiddle_ref,
    mid_ref,
    back_ref,
    hold_ref,
    last_ref,
    sems,
):
    waits = fetch(
        [twiddle_hbm] + [in_hbm.at[:, n] for n in range(8)] + [matrix_hbm],
        [twiddle_ref] + [in_ref.at[:, n] for n in range(8)] + [matrix_ref],
        sems,
    )
    waits[0].wait()
    early = lax.broadcasted_iota(jnp.int32, (8, 128), 1) % 32 < 16
    for n0 in range(8):
        waits[1 + n0].wait()
        for tile in range(2):
            pieces = [
                tuple(in_ref[n1, n0, 16 * c + 8 * tile : 16 * c + 8 * tile + 8, :] for c in range(2))
                for n1 in range(8)
            ]
            for ka, value in enumerate(transform(pieces, -1)):
                hold_ref[0, tile, 0, 8 * ka + n0], hold_ref[0, tile, 1, 8 * ka + n0] = times(value, n0 * ka, 64, -1)

    def waves(ka):
        for tile in range(2):
            pieces = [tuple(hold_ref[0, tile, c, 8 * ka + n0] for c in range(2)) for n0 in range(8)]
            for kb, (real, imag) in enumerate(transform(pieces, -1)):
                m1 = ka + 8 * kb
                tr, ti = twiddle_ref[0, m1 : m1 + 1, :], twiddle_ref[1, m1 : m1 + 1, :]
                at = 128 * ka + 16 * kb + 8 * tile
                mid_ref[at : at + 8, 0:128] = real * tr - imag * ti
                mid_ref[at : at + 8, 128:256] = real * ti + imag * tr

    def turn(pair):
        rows = slice(256 * pair, 256 * pair + 256)
        spectrum = matmul(spread(mid_ref[rows, :]), matrix, ((1,), (0,)))
        real, imag = spectrum[:, :128], spectrum[:, 128:]
        for ref in range(2):
            cosine, sine = shift_ref[2 * ref, rows, :], shift_ref[2 * ref + 1, rows, :]
            turned = jnp.concatenate([real * sine + imag * cosine, real * cosine - imag * sine], axis=1)
            back_ref[ref, rows, :] = matmul(spread(turned), matrix, ((1,), (0,)))

    def back(ka):
        for ref in range(2):
            for tile in range(2):
                pieces = []
                for kb in range(8):
                    m1 = ka + 8 * kb
                    at = 128 * ka + 16 * kb + 8 * tile
                    imag, real = back_ref[ref, at : at + 8, 0:128], back_ref[ref, at : at + 8, 128:256]
                    tr, ti = twiddle_ref[0, m1 : m1 + 1, :], twiddle_ref[1, m1 : m1 + 1, :]
                    pieces.append((real * tr + imag * ti, imag * tr - real * ti))
                for sa, value in enumerate(transform(pieces, 1)):
                    real, imag = times(value, ka * sa, 64, 1)
                    last_ref[ref, tile, 0, 8 * sa + ka], last_ref[ref, tile, 1, 8 * sa + ka] = real, imag

    waits[9].wait()
    matrix = tripled(matrix_ref, 0)
    waves(0)
    waves(1)
    for pair in range(4):
        turn(pair)
        for ka in (2 * pair + 2, 2 * pair + 3):
            if ka < 8:
                waves(ka)
        for ka in (2 * pair - 2, 2 * pair - 1):
            if ka >= 0:
                back(ka)
    back(6)
    back(7)
    leaving = []
    for sa in range(8):
        for tile in range(2):
            both = [
                transform([tuple(last_ref[ref, tile, c, 8 * sa + n0] for c in range(2)) for n0 in range(8)], 1)
                for ref in range(2)
            ]
            for sb in range(8):
                s = sa + 8 * sb
                chosen = jnp.where(early, refs_ref[0, 2 * s], refs_ref[0, 2 * s + 1]) > 0
                for c in range(2):
                    at = slice(16 * c + 8 * tile, 16 * c + 8 * tile + 8)
                    out_ref[sb, sa, at, :] = jnp.where(chosen, both[1][sb][c], both[0][sb][c])
        copy = pltpu.make_async_copy(out_ref.at[:, sa], out_hbm.at[:, sa], sems.at[10 + sa])
        copy.start()
        leaving.append(copy)
    for copy in leaving:
        copy.wait()


def inverse_y_kernel(place_ref, in_ref, phase_ref, coupling_ref, matrix_ref, twiddle_ref, part_ref, *rest):
    first_ref, last_ref, image_refs, mid_ref, image_hold, out_ref = rest[0], rest[1], rest[2:6], *rest[6:]
    matrix = tripled(matrix_ref, 0)
    for p in range(8):
        block = in_ref[8 * p : 8 * p + 8].reshape(256, 128)
        mid_ref[128 * p : 128 * p + 128, :] = matmul(spread(block.T), matrix, ((1,), (0,)))
    for field in range(2):
        for tile in range(4):
            rows = slice(8 * tile, 8 * tile + 8)
            values = []
            for k1 in range(NY_A):
                at = k1 * 64 + field * 32 + tile * 8
                real, imag = mid_ref[at : at + 8, 0:128], mid_ref[at : at + 8, 128:256]
                if k1:
                    tr, ti = twiddle_ref[0, k1 : k1 + 1, :], twiddle_ref[1, k1 : k1 + 1, :]
                    real, imag = real * tr + imag * ti, imag * tr - real * ti
                values.append((real, imag))
            for a, (real, imag) in enumerate(transform(values, 1)):
                lanes = slice(128 * a, 128 * a + 128)
                cosine, sine = phase_ref[0, rows, lanes], phase_ref[1, rows, lanes]
                if field == 0:
                    real, imag = real * cosine + imag * sine, imag * cosine - real * sine
                else:
                    real, imag = real * cosine - imag * sine, imag * cosine + real * sine
                for c, value in enumerate((real, imag)):
                    out_ref[field, c, rows, lanes] = value
                    row = 2 * field + c
                    if tile == 0:
                        first_ref[row : row + 1, lanes] = value[0:1]
                    if tile == 3:
                        last_ref[row : row + 1, lanes] = value[7:8]
    row = lax.broadcasted_iota(jnp.int32, (8, 2048), 0)
    for tile, source, receiver in corrected(out_ref, coupling_ref):
        for field, pair in enumerate((source, receiver)):
            for c in range(2):
                part_ref[field, 0, c, 8 * tile : 8 * tile + 8, :] = pair[c]
        image = source[0] * receiver[0] + source[1] * receiver[1]
        if tile == 0:
            image = jnp.where(row == 0, 0.0, image)
        if tile == 3:
            image = jnp.where(row == 7, 0.0, image)
        image_hold[8 * tile : 8 * tile + 8, :] = image
    place = place_ref[0]
    for k in range(4):
        at = pl.multiple_of(((place + k) % 4) * 8, 8)
        image_refs[k][...] = image_hold[pl.ds(at, 8), :]


def edges_kernel(index_ref, above_ref, below_ref, part_ref, coupling_ref, out_hbm, edge_ref, whole_ref, sems):
    inner = pltpu.make_async_copy(part_ref.at[:, :, :, 8:24, :], out_hbm.at[:, :, :, 8:24, :], sems.at[0])
    inner.start()
    index = jnp.full((1, 2048), index_ref[0], jnp.int32)
    whole_ref[:, :, :, 0] = part_ref[:, :, :, 0:8, :]
    whole_ref[:, :, :, 1] = part_ref[:, :, :, 24:32, :]
    for side, (halo_ref, row, end) in enumerate(((above_ref, 0, 0), (below_ref, 7, 63))):
        coupling = coupling_ref[31 * side : 31 * side + 1, :]
        results = []
        for field in range(2):
            real, imag = (
                jnp.where(index == end, 0.0, halo_ref[2 * field + c : 2 * field + c + 1, :]) for c in range(2)
            )
            scaled = coupling if field else -coupling
            real, imag = (
                whole_ref[field, 0, 0, side, row : row + 1, :] - scaled * imag,
                whole_ref[field, 0, 1, side, row : row + 1, :] + scaled * real,
            )
            whole_ref[field, 0, 0, side, row : row + 1, :] = real
            whole_ref[field, 0, 1, side, row : row + 1, :] = imag
            results.append((real, imag))
        image = results[0][0] * results[1][0] + results[0][1] * results[1][1]
        for part in range(4):
            edge_ref[4 * side + part : 4 * side + part + 1, :] = image[:, 512 * part : 512 * part + 512]
    outer = [
        pltpu.make_async_copy(
            whole_ref.at[:, :, :, side], out_hbm.at[:, :, :, 24 * side : 24 * side + 8, :], sems.at[1 + side]
        )
        for side in range(2)
    ]
    for copy in outer:
        copy.start()
    for copy in [inner] + outer:
        copy.wait()


def corrected(wave_ref, coupling_ref):
    row = lax.broadcasted_iota(jnp.int32, (8, 2048), 0)
    lane = lax.broadcasted_iota(jnp.int32, (8, 2048), 1)
    for tile in range(4):
        rows = slice(8 * tile, 8 * tile + 8)
        coupling = coupling_ref[rows, :]
        results = []
        for field in range(2):
            laplace = []
            for c in range(2):
                value = wave_ref[field, c, rows, :]
                before = wave_ref[field, c, 8 * tile - 1 : 8 * tile, :] if tile > 0 else 0.0
                after = wave_ref[field, c, 8 * tile + 8 : 8 * tile + 9, :] if tile < 3 else 0.0
                up = jnp.where(row == 0, before, pltpu.roll(value, 1, 0))
                down = jnp.where(row == 7, after, pltpu.roll(value, 7, 0))
                left = jnp.where(lane == 0, 0.0, pltpu.roll(value, 1, 1))
                right = jnp.where(lane == 2047, 0.0, pltpu.roll(value, 2047, 1))
                laplace.append(up + down + left + right - 4.0 * value)
            scaled = coupling if field else -coupling
            real = wave_ref[field, 0, rows, :] - scaled * laplace[1]
            imag = wave_ref[field, 1, rows, :] + scaled * laplace[0]
            results.append((real, imag))
        yield tile, results[0], results[1]


def assemble_kernel(place_ref, own_ref, *rest):
    refs, out_ref = (own_ref,) + rest[:3], rest[3]
    place = place_ref[0]
    for k, ref in enumerate(refs):
        at = pl.multiple_of(((place + 4 - k) % 4) * 8, 8)
        out_ref[0, pl.ds(at, 8), :] = ref[:, 0:2048]
    if own_ref.shape[1] > 2048:
        edges = [ref[:, 2048:2560] for ref in refs]
        total = edges[0] + edges[1] + edges[2] + edges[3]
        for part in range(4):
            lanes = slice(512 * part, 512 * part + 512)
            out_ref[0, 0:1, lanes] = total[part : part + 1]
            out_ref[0, 31:32, lanes] = total[4 + part : 5 + part]


def whole(memory=pltpu.VMEM):
    return pl.BlockSpec(memory_space=memory)


def f32(*shape):
    return jax.ShapeDtypeStruct(shape, jnp.float32)


def call(kernel, out_shape, operands, scratch=(), smem=0, far=0, near=(), near_out=False, far_out=False, first_out_far=False):
    hbm = whole(pl.ANY if INTERPRET else pltpu.HBM)
    many = isinstance(out_shape, (tuple, list))
    if not INTERPRET:
        operands = tuple(
            pltpu.with_memory_space_constraint(x, pltpu.VMEM)
            if i in near
            else pltpu.with_memory_space_constraint(x, pltpu.HBM) if i >= len(operands) - far else x
            for i, x in enumerate(operands)
        )
        if near_out:
            shapes = out_shape if many else (out_shape,)
            shapes = tuple(pltpu.VMEM(x.shape, x.dtype) for x in shapes)
            out_shape = shapes if many else shapes[0]
        if first_out_far:
            out_shape = (pltpu.HBM(out_shape[0].shape, out_shape[0].dtype),) + tuple(out_shape[1:])
        if far_out:
            out_shape = pltpu.HBM(out_shape.shape, out_shape.dtype)
    return pl.pallas_call(
        kernel,
        out_shape=out_shape,
        in_specs=[whole(pltpu.SMEM)] * smem
        + [whole()] * (len(operands) - smem - far)
        + [hbm] * far,
        out_specs=(
            [hbm if first_out_far and i == 0 else whole() for i in range(len(out_shape))]
            if many
            else hbm if far_out else whole()
        ),
        scratch_shapes=list(scratch),
        interpret=INTERPRET,
        compiler_params=pltpu.CompilerParams(vmem_limit_bytes=VMEM_BYTES),
    )(*operands)


def forward_y(wavefields):
    const = constants()
    return call(
        forward_y_kernel,
        f32(64, 32, 128),
        (wavefields, jnp.asarray(const["y_matrix"]), jnp.asarray(const["y_twiddle"])),
        (
            pltpu.VMEM((2, 1, 2, 32, 2048), jnp.float32),
            pltpu.VMEM((2, 256, 256), BF16),
            pltpu.VMEM((2, 16, 128), jnp.float32),
            pltpu.VMEM((1024, 256), jnp.float32),
            pltpu.SemaphoreType.DMA((10,)),
        ),
        far=3,
        near_out=True,
    )


def middle(blocks, shift, ref_index):
    const = constants()
    blocks = call(
        middle_kernel,
        f32(8, 8, 32, 128),
        (
            ref_index,
            shift,
            blocks.reshape(8, 8, 32, 128),
            jnp.asarray(const["x_matrix"]),
            jnp.asarray(const["x_twiddle"]),
        ),
        (
            pltpu.VMEM((8, 8, 32, 128), jnp.float32),
            pltpu.VMEM((8, 8, 32, 128), jnp.float32),
            pltpu.VMEM((2, 256, 256), BF16),
            pltpu.VMEM((2, 64, 128), jnp.float32),
            pltpu.VMEM((1024, 256), jnp.float32),
            pltpu.VMEM((2, 1024, 256), jnp.float32),
            pltpu.VMEM((1, 2, 2, 64, 8, 128), jnp.float32),
            pltpu.VMEM((2, 2, 2, 64, 8, 128), jnp.float32),
            pltpu.SemaphoreType.DMA((18,)),
        ),
        smem=1,
        far=3,
        near=(1,),
        far_out=True,
    )
    return blocks.reshape(64, 32, 128)


def inverse_y(place, blocks, phase, coupling):
    const = constants()
    return call(
        inverse_y_kernel,
        (f32(2, 1, 2, 32, 2048),) + (f32(4, 2048),) * 2 + (f32(8, 2048),) * 4,
        (place, blocks, phase, coupling, jnp.asarray(const["y_matrix"]), jnp.asarray(const["y_twiddle"])),
        (
            pltpu.VMEM((1024, 256), jnp.float32),
            pltpu.VMEM((32, 2048), jnp.float32),
            pltpu.VMEM((2, 2, 32, 2048), jnp.float32),
        ),
        smem=1,
        near=(1, 2, 3),
        near_out=True,
    )


def add_edges(index, above, below, part, coupling):
    return call(
        edges_kernel,
        (f32(2, 1, 2, 32, 2048), f32(8, 512)),
        (index, above, below, part, coupling),
        (pltpu.VMEM((2, 1, 2, 2, 8, 2048), jnp.float32), pltpu.SemaphoreType.DMA((3,))),
        smem=1,
        near=(1, 2, 3, 4),
        first_out_far=True,
    )


def assemble(place, pieces):
    return call(assemble_kernel, f32(1, 32, 2048), (place,) + tuple(pieces), smem=1)


def wave_values(number, length):
    signed = jnp.where(number < length // 2, number, number - length)
    return 2.0 * math.pi / length * signed.astype(jnp.float32)


def shift_tables(space_index, omega, ref_velocity):
    row = lax.broadcasted_iota(jnp.int32, (1024, 128), 0)
    lane = lax.broadcasted_iota(jnp.int32, (1024, 128), 1)
    kx = wave_values(row // 128 + 8 * (row // 16 % 8) + 64 * (lane % 32), NX)
    k1 = 2 * (space_index // 8) + lane // 64
    k2 = 16 * (space_index % 8) + row % 16
    ky = wave_values(k1 + 16 * k2, NY)
    sign = jnp.where((lane // 32) % 2 == 0, -1.0, 1.0).astype(jnp.float32)
    squared = kx**2 + ky**2
    tables = []
    for ref in range(2):
        vertical = (omega / ref_velocity[ref]) ** 2 - squared
        root = DZ * jnp.sqrt(jnp.abs(vertical))
        travels = vertical >= 0.0
        tables.append(jnp.where(travels, jnp.cos(root), jnp.exp(-root)))
        tables.append(jnp.where(travels, sign * jnp.sin(root), 0.0))
    return jnp.stack(tables) * (1.0 / NX)


def phase_tables(speed, ref_rows, omega):
    time_shift = omega * DZ * (1.0 / speed - 1.0 / ref_rows)
    return jnp.stack([jnp.cos(time_shift), jnp.sin(time_shift)]) * (1.0 / NY)


def coupling_table(speed, ref_rows, omega):
    return DZ * (speed - ref_rows) * ref_rows / (16.0 * omega)


def shifted_pairs(step, count=4):
    return [(i, (i + step) % count) for i in range(count)]


def slab_speed(velocity, owner, freq_index):
    stored = lax.dynamic_index_in_dim(velocity, owner % 4, 0, keepdims=False).reshape(4, 8, 2048)
    source = owner // 4
    mine = lax.dynamic_index_in_dim(stored, freq_index, 0, keepdims=False)
    for step in (1, 2, 3):
        piece = lax.dynamic_index_in_dim(stored, (freq_index + step) % 4, 0, keepdims=False)
        arrived = lax.ppermute(piece, "freq", shifted_pairs(step))
        mine = jnp.where((freq_index + 4 - step) % 4 == source, arrived, mine)
    return gathered(mine)


def gathered(mine):
    pieces = [mine]
    for step in (1, 2, 3):
        pieces.append(lax.ppermute(mine, "freq", shifted_pairs(step)))
    return pieces


def exchange(blocks):
    return lax.all_to_all(blocks, "space", split_axis=0, concat_axis=0, tiled=True)


def step_down(wavefields, frequencies, velocity, slab_owner, ref_velocity, ref_index):
    space_index = lax.axis_index("space")
    freq_index = lax.axis_index("freq")
    place = freq_index.reshape(1).astype(jnp.int32)
    omega = frequencies[0]
    slab = slab_speed(velocity, slab_owner[0], freq_index)
    blocks = forward_y(wavefields)
    blocks = exchange(blocks)
    shift = shift_tables(space_index, omega, ref_velocity[0])
    speed = assemble(place, slab)[0]
    local_refs = lax.dynamic_slice_in_dim(ref_index[0], 2 * space_index, 2)
    ref_rows = jnp.repeat(ref_velocity[0][local_refs], 16)[:, None]
    phase = phase_tables(speed, ref_rows, omega)
    coupling = coupling_table(speed, ref_rows, omega)
    blocks = middle(blocks, shift, ref_index)
    blocks = exchange(blocks)
    part, first, last, *quarters = inverse_y(place, blocks, phase, coupling)
    above = lax.ppermute(last, "space", shifted_pairs(1, 64))
    below = lax.ppermute(first, "space", shifted_pairs(63, 64))
    total = quarters[0]
    for step in (1, 2, 3):
        arrived = lax.ppermute(quarters[step], "freq", shifted_pairs(step))
        total = total + arrived
    index = space_index.reshape(1).astype(jnp.int32)
    fields, edges = add_edges(index, above, below, part, coupling)
    image = assemble(place, gathered(jnp.concatenate([total, edges], axis=1)))
    return fields, image


def solution(mesh):
    in_specs = (
        P(None, "freq", None, "space", None),
        P("freq"),
        P("freq", "space", None),
        P(),
        P(),
        P(),
    )
    out_specs = (P(None, "freq", None, "space", None), P(None, "space", None))
    return jax.shard_map(step_down, mesh=mesh, in_specs=in_specs, out_specs=out_specs, check_vma=False)
```
